512 devices in a mesh: dp: 64 (over z_lo, y, core), mp: 8 (over x, z_hi).
Axes of the slice: x: 4, y: 8, z: 8 (z_hi: 2, z_lo: 4; z = z_hi * 4 + z_lo), core: 2. Of those that a mesh axis runs over, the one named last changes fastest.
Arguments:
- activations: bfloat16 [65536, 4096], P('dp', 'mp'), may hold values from -6 to 6
- out_grad: bfloat16 [65536, 14336], P('dp', 'mp'), may hold values from -0.0234375 to 0.0234375
- tile_list: int32 [8, 64, 2], P('mp'), may hold values from 0 to 111, as said below
- tile_count: int32 [8], P('mp'), may hold values from 32 to 64, as said below
Outputs:
- grad_tiles: float32 [8, 64, 128, 128], P('mp', 'dp')
The draws below stay inside these ranges and needn't reach their ends.
Inputs may be any that keep to these rules, and one draw needn't show every extreme that they name: `tile_list`: in shard c the 64 entries name distinct blocks; the block row lies in 0 to 31 and the block column in c * 14 to (c + 1) * 14 - 1. `tile_count`: some shard has all 64 slots live.
All inputs are finite; a program needn't handle non-finite values.
Results may differ from the reference program's by a relative error of at most 0.0003.
Values may be sent and summed in bfloat16 or wider, within the bound.
A program may use at most 128 MiB of HBM per device.

```python
import jax
import jax.numpy as jnp
from jax import lax

D = 4096
FF = 14336
BLK = 128
SLOTS = 1
TOKENS = 65536
N_DP = 64
N_MP = 8


def draw_tile_list(key, part):
    per_shard = FF // (N_MP * BLK)
    block_total = D // BLK * per_shard
    slot_total = N_DP * SLOTS

    def one_shard(shard_id):
        shuffled = jax.random.permutation(jax.random.fold_in(key, shard_id), block_total)[:slot_total]
        return jnp.stack([shuffled // per_shard, shard_id * per_shard + shuffled % per_shard], axis=-1)
    return jax.vmap(one_shard)(jnp.arange(N_MP, dtype=jnp.int32)).astype(jnp.int32)


def draw_tile_count(key, part):
    slot_total = N_DP * SLOTS
    lowest = slot_total // 2
    counts = jax.random.randint(jax.random.fold_in(key, 11), (N_MP,), lowest, slot_total + 1)
    fullest = jax.random.randint(jax.random.fold_in(key, 12), (), 0, N_MP)
    positions = jnp.arange(N_MP, dtype=jnp.int32)
    counts = jnp.where(positions == fullest, slot_total, counts)
    counts = jnp.where(positions == (fullest + 1) % N_MP, lowest, counts)
    return counts.astype(jnp.int32)


def level_of(rng, shape, cuts, low, high):
    loudness = 1.0
    for axis_at, shards_of in cuts:
        heights = jax.random.uniform(jax.random.fold_in(jax.random.fold_in(rng, 6), axis_at), (shards_of,), jnp.float32, low / len(cuts), high / len(cuts))
        loudness = loudness * jnp.repeat(jnp.exp(heights), shape[axis_at] // shards_of).reshape((-1,) + (1,) * (len(shape) - 1 - axis_at))
    return loudness


def normal_values(key, extent, spread, reach, split=(), held_as=jnp.bfloat16):
    values = spread * jax.random.normal(key, extent, jnp.float32)
    if split:
        values = values * level_of(key, extent, split, -0.22, 0.18)
    return jnp.clip(values, -reach, reach).astype(held_as)


def setup_inputs(seed: int = 0) -> dict:
    splits = jax.random.split(jax.random.key(seed), 5)
    return {
        "activations": normal_values(splits[0], (TOKENS, D), 1.0, 6.0, ((0, 64), (1, 8))),
        "out_grad": normal_values(splits[1], (TOKENS, FF), (1.0 / TOKENS ** 0.5), 0.0234375, ((0, 64), (1, 8))),
        "tile_list": draw_tile_list(jax.random.fold_in(splits[4], 71), 0),
        "tile_count": draw_tile_count(jax.random.fold_in(splits[4], 71), 0),
    }


def reference(activations, out_grad, tile_list, tile_count):
    slot_total = tile_list.shape[1]
    flat_list = tile_list.reshape(-1, 2).astype(jnp.int32)
    shard_ids = jnp.repeat(jnp.arange(N_MP, dtype=jnp.int32), slot_total)
    slot_ids = jnp.tile(jnp.arange(slot_total, dtype=jnp.int32), N_MP)

    def tile_product(entry):
        row_block, col_block, shard_id, slot_id = entry
        act_cols = lax.dynamic_slice_in_dim(activations, (row_block * BLK).astype(jnp.int32), BLK, 1)
        grad_cols = lax.dynamic_slice_in_dim(out_grad, (col_block * BLK).astype(jnp.int32), BLK, 1)
        product = jnp.dot(act_cols.T, grad_cols, preferred_element_type=jnp.float32)
        return jnp.where(slot_id < tile_count[shard_id], product, jnp.zeros_like(product))

    products = lax.map(tile_product, (flat_list[:, 0], flat_list[:, 1], shard_ids, slot_ids))
    return products.reshape(N_MP, slot_total, BLK, BLK)
```

```python
import jax
import jax.numpy as jnp
from jax import lax
from jax.experimental import pallas as pl
from jax.experimental.pallas import tpu as pltpu
from jax.sharding import PartitionSpec as P

MESH = pl.DeviceIdType.MESH
BLK = 128
NX, NY, NZL = 4, 8, 4
T = 4


def rem(a, b):
    return lax.rem(a, jnp.int32(b))


def div(a, b):
    return lax.div(a, jnp.int32(b))


def kernel(tl, act, grad, out, *scratch):
    gath = scratch[:T]
    gbuf, acc, crecv, yrp, yrm, zrecv, lsem, gsem, ssem, rsem = scratch[T:]
    tokens, feats = act.shape
    ch = tokens // T
    hf = ch // 2
    cols = grad.shape[1] // BLK
    per = feats // BLK

    dp, mp = lax.axis_index("dp"), lax.axis_index("mp")
    core, y, zl = rem(dp, 2), rem(div(dp, 2), NY), div(dp, 2 * NY)
    x, zh = div(mp, 2), rem(mp, 2)

    def dev(x_, y_, zl_, zh_, core_):
        return ((zl_ * NY + y_) * 2 + core_, x_ * 2 + zh_)

    xr, xl = rem(x + 1, NX), rem(x + NX - 1, NX)
    right, left = dev(xr, y, zl, zh, core), dev(xl, y, zl, zh, core)
    across = dev(x, y, zl, 1 - zh, core)
    twin = dev(x, y, zl, zh, 1 - core)
    up, down = dev(x, rem(y + 1, NY), zl, zh, core), dev(x, rem(y + NY - 1, NY), zl, zh, core)

    loc_a = []
    for t in range(T):
        for b in range(per):
            c = pltpu.make_async_copy(
                act.at[pl.ds(t * ch, ch), pl.ds(b * BLK, BLK)], gath[t].at[mp * per + b], lsem.at[t, b])
            c.start()
            loc_a.append(c)
    loc_g = []
    for q in range(cols):
        c = pltpu.make_async_copy(grad.at[:, pl.ds(q * BLK, BLK)], gbuf.at[q], gsem.at[q])
        c.start()
        loc_g.append(c)

    barrier = pltpu.get_barrier_semaphore()
    peers = [right, left, across, twin, up, down]
    peers += [dev(x, y, rem(zl + d, NZL), zh, core) for d in range(1, NZL)]
    for p in peers:
        pl.semaphore_signal(barrier, inc=1, device_id=p, device_id_type=MESH)
    pl.semaphore_wait(barrier, len(peers))

    sends = []
    names = {}

    def sem_of(name):
        return names.setdefault(name, len(names))

    def send(name, src, dst, to):
        i = sem_of(name)
        c = pltpu.make_async_remote_copy(
            src_ref=src, dst_ref=dst, send_sem=ssem.at[i], recv_sem=rsem.at[i],
            device_id=to, device_id_type=MESH)
        c.start()
        sends.append(c)

    def arrived(name, dst):
        i = sem_of(name)
        pltpu.make_async_remote_copy(
            src_ref=dst, dst_ref=dst, send_sem=ssem.at[i], recv_sem=rsem.at[i],
            device_id=twin, device_id_type=MESH).wait_recv()

    other = x * 2 + 1 - zh

    def rows(t, h, m):
        return gath[t].at[pl.ds(m * per, per), pl.ds(h * hf, hf)]

    def whole(t, m):
        return gath[t].at[pl.ds(m * per, per)]

    def spread(side, t, m):
        for h in (0, 1):
            for d, to in ((0, right), (1, left)):
                g = h if d == 0 else 1 - h
                send((side, t, d, g), rows(t, g, m), rows(t, g, m), to)

    def pass_on(side, t, z):
        for d, m, to in ((0, xl * 2 + z, right), (1, xr * 2 + z, left)):
            arrived((side, t, d, d), rows(t, d, m))
            send((side, t, d, "on"), rows(t, d, m), rows(t, d, m), to)

    def rest(side, t, z):
        far = rem(x + 2, NX) * 2 + z
        for d, m in ((0, xl * 2 + z), (1, xr * 2 + z)):
            arrived((side, t, d, 1 - d), rows(t, 1 - d, m))
            arrived((side, t, d, "on"), rows(t, d, far))

    def product(t, cr, dy, zp):
        zt = (3 * zp) % 4
        k = (zt * NY + rem(y + dy, NY)) * 2 + rem(core + cr, 2)
        a = gath[t][tl[0, 0, k]]
        g = gbuf[rem(tl[0, 1, k], cols), pl.ds(t * ch, ch)]
        return lax.dot_general(a, g, (((0,), (0,)), ((), ())), preferred_element_type=jnp.float32)

    def group(t, cr, dy):
        for zp in range(4):
            p = product(t, cr, dy, zp)
            acc[cr, dy, zp] = p if t == 0 else acc[cr, dy, zp] + p

    def multiply(t):
        @pl.loop(0, 16)
        def _(i):
            group(t, div(i, 8), rem(i, 8))

    for c in loc_a:
        c.wait()
    for t in range(T):
        send(("z", t), whole(t, mp), whole(t, mp), across)
    for t in range(T):
        spread("own", t, mp)
    for c in loc_g:
        c.wait()
    for t in range(T):
        pass_on("own", t, zh)
        arrived(("z", t), whole(t, other))
        spread("par", t, other)
        if t >= 1:
            pass_on("par", t - 1, 1 - zh)
        if t >= 2:
            rest("own", t - 2, zh)
            rest("par", t - 2, 1 - zh)
            multiply(t - 2)
    pass_on("par", T - 1, 1 - zh)
    for t in (T - 2, T - 1):
        rest("own", t, zh)
        rest("par", t, 1 - zh)
        if t < T - 1:
            multiply(t)

    lo, hi = pl.ds(0, 2), pl.ds(2, 2)

    def last(dy):
        group(T - 1, 1, dy)
        send(("core", dy), acc.at[1, dy], crecv.at[dy], twin)
        group(T - 1, 0, dy)

    def ready(dy):
        arrived(("core", dy), crecv.at[dy])
        acc[0, dy] = acc[0, dy] + crecv[dy]

    def step(plus, dist, half, add):
        buf, to = (yrp, up) if plus else (yrm, down)
        dy = dist if plus else (NY - dist) % NY
        part = lo if half == 0 else hi
        if add:
            arrived(("y", plus, dist, half), buf.at[dist, part])
            acc[0, dy, part] = acc[0, dy, part] + buf[dist, part]
        if dist:
            send(("y", plus, dist - 1, half), acc.at[0, dy, part], buf.at[dist - 1, part], to)

    last(4)
    last(3)
    ready(4)
    step(True, 4, 1, False)
    step(False, 4, 0, False)
    last(5)
    ready(3)
    step(True, 3, 0, False)
    last(2)
    ready(5)
    step(False, 3, 1, False)
    last(6)
    step(True, 3, 1, True)
    step(False, 3, 0, True)
    ready(2)
    step(True, 2, 0, True)
    last(1)
    ready(6)
    step(False, 2, 1, True)
    last(7)
    step(True, 2, 1, True)
    step(False, 2, 0, True)
    ready(1)
    step(True, 1, 0, True)
    last(0)
    ready(7)
    step(False, 1, 1, True)
    step(True, 1, 1, True)
    step(False, 1, 0, True)
    ready(0)

    zsends = []
    zbase = len(names)
    for half in (0, 1):
        step(True, 0, half, True)
        step(False, 0, half, True)
        for zp in (2 * half, 2 * half + 1):
            zt = (3 * zp) % 4
            slot = rem(zl - zt + NZL, NZL)
            c = pltpu.make_async_remote_copy(
                src_ref=acc.at[0, 0, zp], dst_ref=zrecv.at[slot], send_sem=ssem.at[zbase + zp],
                recv_sem=rsem.at[zbase + slot], device_id=dev(x, y, zt, zh, core), device_id_type=MESH)
            pl.when(zl != zt)(c.start)
            zsends.append((zt, c))
    total = acc[0, 0, rem(3 * zl, 4)]
    for slot in range(1, NZL):
        pltpu.make_async_remote_copy(
            src_ref=zrecv.at[slot], dst_ref=zrecv.at[slot], send_sem=ssem.at[zbase],
            recv_sem=rsem.at[zbase + slot], device_id=twin, device_id_type=MESH).wait_recv()
        total = total + zrecv[slot]
    out[0, 0] = total

    for c in sends:
        c.wait_send()
    for zt, c in zsends:
        pl.when(zl != zt)(c.wait_send)
    assert zbase + NZL <= 100


def on_device(activations, out_grad, tile_list, tile_count):
    tokens, feats = activations.shape
    n_mp = NX * 2
    ch = tokens // T
    tile = (BLK, BLK)
    tiles = pl.pallas_call(
        kernel,
        out_shape=jax.ShapeDtypeStruct((1, 1, *tile), jnp.float32),
        in_specs=[
            pl.BlockSpec(memory_space=pltpu.SMEM),
            pl.BlockSpec(memory_space=pl.ANY),
            pl.BlockSpec(memory_space=pl.ANY),
        ],
        out_specs=pl.BlockSpec(memory_space=pltpu.VMEM),
        scratch_shapes=[pltpu.VMEM((n_mp * feats // BLK, ch, BLK), jnp.bfloat16) for _ in range(T)]
        + [
            pltpu.VMEM((out_grad.shape[1] // BLK, tokens, BLK), jnp.bfloat16),
            pltpu.VMEM((2, NY, NZL, *tile), jnp.float32),
            pltpu.VMEM((NY, NZL, *tile), jnp.float32),
            pltpu.VMEM((4, NZL, *tile), jnp.float32),
            pltpu.VMEM((4, NZL, *tile), jnp.float32),
            pltpu.VMEM((NZL, *tile), jnp.float32),
            pltpu.SemaphoreType.DMA((T, feats // BLK)),
            pltpu.SemaphoreType.DMA((out_grad.shape[1] // BLK,)),
            pltpu.SemaphoreType.DMA((100,)),
            pltpu.SemaphoreType.DMA((100,)),
        ],
        compiler_params=pltpu.CompilerParams(
            collective_id=0, has_side_effects=True, vmem_limit_bytes=62 * 1024 * 1024
        ),
    )(jnp.swapaxes(tile_list, 1, 2), activations, out_grad)
    return jnp.where(lax.axis_index("dp") < tile_count[0], tiles, 0.0)


def solution(mesh):
    placed = (P("dp", "mp"), P("dp", "mp"), P("mp", None, None), P("mp"))
    return jax.shard_map(
        on_device, mesh=mesh, in_specs=placed, out_specs=P("mp", "dp", None, None), check_vma=False
    )
```

```python
import jax
import jax.numpy as jnp
from jax import lax
from jax.experimental import pallas as pl
from jax.experimental.pallas import tpu as pltpu
from jax.sharding import PartitionSpec as P

MESH = pl.DeviceIdType.MESH
BLK = 128
NX, NY, NZL = 4, 8, 4
T = 4


RANGE = 32000.0
CODE = BLK + 8


def encode(tiles):
    codes, exps = [], []
    for v in tiles:
        rows = v.reshape(BLK // 8, 8, BLK)
        peak = jnp.max(jnp.abs(rows), axis=0)
        e = jnp.ceil(jnp.log2(jnp.maximum(peak, 1e-30)))
        q = jnp.round(rows * (RANGE * jnp.exp2(-e))[None])
        codes.append(q.reshape(BLK, BLK))
        exps.append(e)
    if len(exps) == 1:
        exps = exps * 2
    return jnp.concatenate(codes + exps, axis=0).astype(jnp.int32).astype(jnp.int16)


def decode(code, n):
    v = code.astype(jnp.int32).astype(jnp.float32)
    out = []
    for i in range(n):
        e = v[n * BLK + 8 * i : n * BLK + 8 * i + 8]
        rows = v[i * BLK : (i + 1) * BLK].reshape(BLK // 8, 8, BLK)
        out.append((rows * (jnp.exp2(e) * (1.0 / RANGE))[None]).reshape(BLK, BLK))
    return out


def rem(a, b):
    return lax.rem(a, jnp.int32(b))


def div(a, b):
    return lax.div(a, jnp.int32(b))


def kernel(tl, act, grad, out, *scratch):
    gath = scratch[:T]
    gbuf, acc, csend, crecv, ysend, yrecv, zsend, zrecv, lsem, gsem, ssem, rsem = scratch[T:]
    tokens, feats = act.shape
    ch = tokens // T
    hf = ch // 2
    cols = grad.shape[1] // BLK
    per = feats // BLK

    dp, mp = lax.axis_index("dp"), lax.axis_index("mp")
    core, y, zl = rem(dp, 2), rem(div(dp, 2), NY), div(dp, 2 * NY)
    x, zh = div(mp, 2), rem(mp, 2)

    def dev(x_, y_, zl_, zh_, core_):
        return ((zl_ * NY + y_) * 2 + core_, x_ * 2 + zh_)

    xr, xl = rem(x + 1, NX), rem(x + NX - 1, NX)
    right, left = dev(xr, y, zl, zh, core), dev(xl, y, zl, zh, core)
    across = dev(x, y, zl, 1 - zh, core)
    twin = dev(x, y, zl, zh, 1 - core)
    up, down = dev(x, rem(y + 1, NY), zl, zh, core), dev(x, rem(y + NY - 1, NY), zl, zh, core)

    barrier = pltpu.get_barrier_semaphore()
    peers = [right, left, across, twin, up, down]
    peers += [dev(x, y, rem(zl + d, NZL), zh, core) for d in range(1, NZL)]
    for p in peers:
        pl.semaphore_signal(barrier, inc=1, device_id=p, device_id_type=MESH)

    loc_a = []
    for t in range(T):
        for b in range(per):
            c = pltpu.make_async_copy(
                act.at[pl.ds(t * ch, ch), pl.ds(b * BLK, BLK)], gath[t].at[mp * per + b], lsem.at[t, b])
            c.start()
            loc_a.append(c)
    loc_g = []
    for q in range(cols):
        c = pltpu.make_async_copy(grad.at[:, pl.ds(q * BLK, BLK)], gbuf.at[q], gsem.at[q])
        c.start()
        loc_g.append(c)

    pl.semaphore_wait(barrier, len(peers))

    sends = []
    names = {}

    def sem_of(name):
        return names.setdefault(name, len(names))

    def send(name, src, dst, to):
        i = sem_of(name)
        c = pltpu.make_async_remote_copy(
            src_ref=src, dst_ref=dst, send_sem=ssem.at[i], recv_sem=rsem.at[i],
            device_id=to, device_id_type=MESH)
        c.start()
        sends.append(c)

    def arrived(name, dst):
        i = sem_of(name)
        pltpu.make_async_remote_copy(
            src_ref=dst, dst_ref=dst, send_sem=ssem.at[i], recv_sem=rsem.at[i],
            device_id=twin, device_id_type=MESH).wait_recv()

    other = x * 2 + 1 - zh

    def rows(t, h, m):
        return gath[t].at[pl.ds(m * per, per), pl.ds(h * hf, hf)]

    def whole(t, m):
        return gath[t].at[pl.ds(m * per, per)]

    def spread(side, t, m):
        for h in (0, 1):
            for d, to in ((0, right), (1, left)):
                g = h if d == 0 else 1 - h
                send((side, t, d, g), rows(t, g, m), rows(t, g, m), to)

    def pass_on(side, t, z):
        for d, m, to in ((0, xl * 2 + z, right), (1, xr * 2 + z, left)):
            arrived((side, t, d, d), rows(t, d, m))
            send((side, t, d, "on"), rows(t, d, m), rows(t, d, m), to)

    def rest(side, t, z):
        far = rem(x + 2, NX) * 2 + z
        for d, m in ((0, xl * 2 + z), (1, xr * 2 + z)):
            arrived((side, t, d, 1 - d), rows(t, 1 - d, m))
            arrived((side, t, d, "on"), rows(t, d, far))

    def product(t, cr, dy, zp):
        zt = (3 * zp) % 4
        k = (zt * NY + rem(y + dy, NY)) * 2 + rem(core + cr, 2)
        a = gath[t][tl[0, 0, k]]
        g = gbuf[rem(tl[0, 1, k], cols), pl.ds(t * ch, ch)]
        return lax.dot_general(a, g, (((0,), (0,)), ((), ())), preferred_element_type=jnp.float32)

    def group(t, cr, dy):
        for zp in range(4):
            p = product(t, cr, dy, zp)
            acc[cr, dy, zp] = p if t == 0 else acc[cr, dy, zp] + p

    def multiply(t):
        @pl.loop(0, 16)
        def _(i):
            group(t, div(i, 8), rem(i, 8))

    for c in loc_a:
        c.wait()
    for t in range(T):
        send(("z", t), whole(t, mp), whole(t, mp), across)
    for t in range(T):
        spread("own", t, mp)
    for c in loc_g:
        c.wait()
    for t in range(T):
        pass_on("own", t, zh)
        arrived(("z", t), whole(t, other))
        spread("par", t, other)
        if t >= 1:
            pass_on("par", t - 1, 1 - zh)
        if t >= 2:
            rest("own", t - 2, zh)
            rest("par", t - 2, 1 - zh)
            multiply(t - 2)
    pass_on("par", T - 1, 1 - zh)
    for t in (T - 2, T - 1):
        rest("own", t, zh)
        rest("par", t, 1 - zh)
        if t < T - 1:
            multiply(t)

    def last(dy):
        group(T - 1, 1, dy)
        for h in (0, 1):
            csend[dy, h] = encode([acc[1, dy, 2 * h], acc[1, dy, 2 * h + 1]])
        send(("core", dy), csend.at[dy], crecv.at[dy], twin)
        group(T - 1, 0, dy)

    def add(dy, half, code):
        for zp, v in zip((2 * half, 2 * half + 1), decode(code, 2)):
            acc[0, dy, zp] = acc[0, dy, zp] + v

    def ready(dy):
        arrived(("core", dy), crecv.at[dy])
        for h in (0, 1):
            add(dy, h, crecv[dy, h])

    def step(plus, dist, half, join):
        way, to = (0, up) if plus else (1, down)
        dy = dist if plus else (NY - dist) % NY
        if join:
            arrived(("y", plus, dist, half), yrecv.at[way, dist, half])
            add(dy, half, yrecv[way, dist, half])
        if dist:
            ysend[way, dist - 1, half] = encode([acc[0, dy, 2 * half], acc[0, dy, 2 * half + 1]])
            send(("y", plus, dist - 1, half), ysend.at[way, dist - 1, half], yrecv.at[way, dist - 1, half], to)

    last(4)
    last(3)
    ready(4)
    step(True, 4, 1, False)
    step(False, 4, 0, False)
    last(5)
    ready(3)
    step(True, 3, 0, False)
    last(2)
    ready(5)
    step(False, 3, 1, False)
    last(6)
    step(True, 3, 1, True)
    step(False, 3, 0, True)
    ready(2)
    step(True, 2, 0, True)
    last(1)
    ready(6)
    step(False, 2, 1, True)
    last(7)
    step(True, 2, 1, True)
    step(False, 2, 0, True)
    ready(1)
    step(True, 1, 0, True)
    last(0)
    ready(7)
    step(False, 1, 1, True)
    step(True, 1, 1, True)
    step(False, 1, 0, True)
    ready(0)

    zsends = []
    zbase = len(names)
    for half in (0, 1):
        step(True, 0, half, True)
        step(False, 0, half, True)
        for zp in (2 * half, 2 * half + 1):
            zt = (3 * zp) % 4
            slot = rem(zl - zt + NZL, NZL)
            zsend[zp] = encode([acc[0, 0, zp]])
            c = pltpu.make_async_remote_copy(
                src_ref=zsend.at[zp], dst_ref=zrecv.at[slot], send_sem=ssem.at[zbase + zp],
                recv_sem=rsem.at[zbase + slot], device_id=dev(x, y, zt, zh, core), device_id_type=MESH)
            pl.when(zl != zt)(c.start)
            zsends.append((zt, c))
    total = acc[0, 0, rem(3 * zl, 4)]
    for slot in range(1, NZL):
        pltpu.make_async_remote_copy(
            src_ref=zrecv.at[slot], dst_ref=zrecv.at[slot], send_sem=ssem.at[zbase],
            recv_sem=rsem.at[zbase + slot], device_id=twin, device_id_type=MESH).wait_recv()
        total = total + decode(zrecv[slot], 1)[0]
    out[0, 0] = total

    for c in sends:
        c.wait_send()
    for zt, c in zsends:
        pl.when(zl != zt)(c.wait_send)
    assert zbase + NZL <= 100


def on_device(activations, out_grad, tile_list, tile_count):
    tokens, feats = activations.shape
    n_mp = NX * 2
    ch = tokens // T
    tile = (BLK, BLK)
    tiles = pl.pallas_call(
        kernel,
        out_shape=jax.ShapeDtypeStruct((1, 1, *tile), jnp.float32),
        in_specs=[
            pl.BlockSpec(memory_space=pltpu.SMEM),
            pl.BlockSpec(memory_space=pl.ANY),
            pl.BlockSpec(memory_space=pl.ANY),
        ],
        out_specs=pl.BlockSpec(memory_space=pltpu.VMEM),
        scratch_shapes=[pltpu.VMEM((n_mp * feats // BLK, ch, BLK), jnp.bfloat16) for _ in range(T)]
        + [
            pltpu.VMEM((out_grad.shape[1] // BLK, tokens, BLK), jnp.bfloat16),
            pltpu.VMEM((2, NY, NZL, *tile), jnp.float32),
            pltpu.VMEM((NY, 2, 2 * CODE, BLK), jnp.int16),
            pltpu.VMEM((NY, 2, 2 * CODE, BLK), jnp.int16),
            pltpu.VMEM((2, 4, 2, 2 * CODE, BLK), jnp.int16),
            pltpu.VMEM((2, 4, 2, 2 * CODE, BLK), jnp.int16),
            pltpu.VMEM((NZL, BLK + 16, BLK), jnp.int16),
            pltpu.VMEM((NZL, BLK + 16, BLK), jnp.int16),
            pltpu.SemaphoreType.DMA((T, feats // BLK)),
            pltpu.SemaphoreType.DMA((out_grad.shape[1] // BLK,)),
            pltpu.SemaphoreType.DMA((100,)),
            pltpu.SemaphoreType.DMA((100,)),
        ],
        compiler_params=pltpu.CompilerParams(
            collective_id=0, has_side_effects=True, vmem_limit_bytes=62 * 1024 * 1024
        ),
    )(jnp.swapaxes(tile_list, 1, 2), activations, out_grad)
    return jnp.where(lax.axis_index("dp") < tile_count[0], tiles, 0.0)


def solution(mesh):
    placed = (P("dp", "mp"), P("dp", "mp"), P("mp", None, None), P("mp"))
    return jax.shard_map(
        on_device, mesh=mesh, in_specs=placed, out_specs=P("mp", "dp", None, None), check_vma=False
    )
```

```python
import jax
import jax.numpy as jnp
from jax import lax
from jax.experimental import pallas as pl
from jax.experimental.pallas import tpu as pltpu
from jax.sharding import PartitionSpec as P

MESH = pl.DeviceIdType.MESH
BLK = 128
NX, NY, NZL = 4, 8, 4
T = 4
NSEM = 65


RANGE = 32000.0
CODE = BLK + 16


def encode(v):
    rows = v.reshape(BLK // 16, 16, BLK)
    peak = jnp.max(jnp.abs(rows), axis=0)
    e = jnp.ceil(jnp.log2(jnp.maximum(peak, 1e-30)))
    q = jnp.round(rows * (RANGE * jnp.exp2(-e))[None])
    return jnp.concatenate([q.reshape(BLK, BLK), e], axis=0).astype(jnp.int32).astype(jnp.int16)


def decode(code):
    v = code.astype(jnp.int32).astype(jnp.float32)
    scale = jnp.exp2(v[BLK:]) * (1.0 / RANGE)
    return (v[:BLK].reshape(BLK // 16, 16, BLK) * scale[None]).reshape(BLK, BLK)


def rem(a, b):
    return lax.rem(a, jnp.int32(b))


def div(a, b):
    return lax.div(a, jnp.int32(b))


def kernel(tl, act, grad, out, *scratch):
    gath = scratch[:T]
    araw, gbuf, acc, csend, crecv, ysend, yrecv, zsend, zrecv, lsem, ssem, rsem = scratch[T:]
    tokens, feats = act.shape
    ch = tokens // T
    hf = ch // 2
    cols = grad.shape[1] // BLK
    per = feats // BLK

    dp, mp = lax.axis_index("dp"), lax.axis_index("mp")
    core, y, zl = rem(dp, 2), rem(div(dp, 2), NY), div(dp, 2 * NY)
    x, zh = div(mp, 2), rem(mp, 2)

    def dev(x_, y_, zl_, zh_, core_):
        return ((zl_ * NY + y_) * 2 + core_, x_ * 2 + zh_)

    xr, xl = rem(x + 1, NX), rem(x + NX - 1, NX)
    right, left = dev(xr, y, zl, zh, core), dev(xl, y, zl, zh, core)
    across = dev(x, y, zl, 1 - zh, core)
    twin = dev(x, y, zl, zh, 1 - core)
    up, down = dev(x, rem(y + 1, NY), zl, zh, core), dev(x, rem(y + NY - 1, NY), zl, zh, core)

    barrier = pltpu.get_barrier_semaphore()
    peers = [across, right, left, twin, up, down]
    peers += [dev(x, y, rem(zl + d, NZL), zh, core) for d in range(1, NZL)]
    for p in peers:
        pl.semaphore_signal(barrier, inc=1, device_id=p, device_id_type=MESH)

    loc = []
    for t in range(T):
        c = pltpu.make_async_copy(act.at[pl.ds(t * ch, ch)], araw.at[pl.ds(t * ch, ch)], lsem.at[t])
        c.start()
        loc.append(c)
    for q in range(cols):
        pltpu.make_async_copy(grad.at[:, pl.ds(q * BLK, BLK)], gbuf.at[q], lsem.at[T]).start()
    for t in range(T):
        loc[t].wait()
        for h in (0, 1):
            for b in range(per):
                part = araw[t * ch + h * hf : t * ch + (h + 1) * hf, b * BLK : (b + 1) * BLK]
                gath[t][mp * per + b, h] = part.T
    pl.semaphore_wait(barrier, len(peers))

    names = {}

    def send(group, name, src, dst, to):
        i = names.setdefault(name, len(names))
        pltpu.make_async_remote_copy(
            src_ref=src, dst_ref=dst, send_sem=ssem.at[group], recv_sem=rsem.at[i],
            device_id=to, device_id_type=MESH).start()

    def arrived(name, dst):
        i = names.setdefault(name, len(names))
        pltpu.make_async_remote_copy(
            src_ref=dst, dst_ref=dst, send_sem=ssem.at[0], recv_sem=rsem.at[i],
            device_id=twin, device_id_type=MESH).wait_recv()

    def sent(group, ref):
        pltpu.make_async_remote_copy(
            src_ref=ref, dst_ref=ref, send_sem=ssem.at[group], recv_sem=rsem.at[0],
            device_id=twin, device_id_type=MESH).wait_send()

    def rows(t, h, m):
        return gath[t].at[pl.ds(m * per, per), h]

    def whole(t, m):
        return gath[t].at[pl.ds(m * per, per)]

    def spread(side, t, m):
        for h in (0, 1):
            for d, to in ((0, right), (1, left)):
                g = h if d == 0 else 1 - h
                name = (side, t, d) if h == 0 else (side, t)
                send(t, name, rows(t, g, m), rows(t, g, m), to)

    def pass_on(side, t):
        z = zh if side == "own" else 1 - zh
        for d, m, to in ((0, xl * 2 + z, right), (1, xr * 2 + z, left)):
            arrived((side, t, d), rows(t, d, m))
            send(t, (side, t), rows(t, d, m), rows(t, d, m), to)

    def rest(t):
        for side in ("own", "par"):
            arrived((side, t), gath[t].at[pl.ds(0, 2 * per)])

    def cross(t):
        m = x * 2 + 1 - zh
        arrived(("z", t), whole(t, m))
        spread("par", t, m)

    def group(t, cr, dy):
        for zp in range(NZL):
            zt = (3 * zp) % NZL
            k = (zt * NY + rem(y + dy, NY)) * 2 + rem(core + cr, 2)
            a = gath[t][tl[0, 0, k]]
            g = gbuf[rem(tl[0, 1, k], cols), pl.ds(t * ch, ch)]
            p = jnp.dot(jnp.concatenate([a[0], a[1]], axis=1), g, preferred_element_type=jnp.float32)
            acc[cr, dy, zp] = p if t == 0 else acc[cr, dy, zp] + p

    def multiply(t):
        @pl.loop(0, 2 * NY)
        def _(i):
            group(t, div(i, NY), rem(i, NY))

    for t in range(T):
        send(t, ("z", t), whole(t, mp), whole(t, mp), across)
    for t in range(T):
        spread("own", t, mp)
    for t in range(T):
        pass_on("own", t)
    pltpu.make_async_copy(gbuf, gbuf, lsem.at[T]).wait()
    cross(0)
    cross(1)
    pass_on("par", 0)
    cross(2)
    pass_on("par", 1)
    rest(0)
    multiply(0)
    pass_on("par", 2)
    cross(3)
    rest(1)
    multiply(1)
    pass_on("par", 3)
    rest(2)
    multiply(2)
    rest(3)

    def last(dy):
        group(T - 1, 1, dy)
        for zp in range(NZL):
            csend[dy, zp] = encode(acc[1, dy, zp])
        send(T, ("core", dy), csend.at[dy], crecv.at[dy], twin)
        group(T - 1, 0, dy)

    def ready(dy):
        arrived(("core", dy), crecv.at[dy])
        for zp in range(NZL):
            acc[0, dy, zp] = acc[0, dy, zp] + decode(crecv[dy, zp])

    def step(way, dist, zp):
        dy = dist if way == 0 else (NY - dist) % NY
        long = (zp >= 2) == (way == 0)
        v = acc[0, dy, zp]
        if dist < (4 if long else 3):
            arrived(("y", way, dist, zp), yrecv.at[way, dist, zp])
            v = v + decode(yrecv[way, dist, zp])
        ysend[way, (4 - dist) * NZL + (zp + 2 * (1 - way)) % NZL] = encode(v)
        send(
            T + 1 + way, ("y", way, dist - 1, zp),
            ysend.at[way, (4 - dist) * NZL + (zp + 2 * (1 - way)) % NZL],
            yrecv.at[way, dist - 1, zp], (up, down)[way])

    def steps(dist, part):
        for i in (0, 1):
            for way in (0, 1):
                step(way, dist, 2 * (part if way == 0 else 1 - part) + i)

    last(4)
    last(3)
    ready(4)
    steps(4, 1)
    last(5)
    ready(3)
    ready(5)
    steps(3, 0)
    last(2)
    last(6)
    steps(3, 1)
    ready(2)
    ready(6)
    steps(2, 0)
    last(1)
    last(7)
    steps(2, 1)
    ready(1)
    ready(7)
    steps(1, 0)
    last(0)
    steps(1, 1)
    ready(0)

    zs = T + 3
    for part in (0, 1):
        for zp in (2 * part, 2 * part + 1):
            v = acc[0, 0, zp]
            for way in (0, 1):
                arrived(("y", way, 0, zp), yrecv.at[way, 0, zp])
                v = v + decode(yrecv[way, 0, zp])
            acc[0, 0, zp] = v
            zt = (3 * zp) % NZL
            slot = rem(zl - zt + NZL, NZL)
            zsend[zp] = encode(v)
            i = names.setdefault("line", len(names))
            c = pltpu.make_async_remote_copy(
                src_ref=zsend.at[zp], dst_ref=zrecv.at[slot], send_sem=ssem.at[zs],
                recv_sem=rsem.at[i], device_id=dev(x, y, zt, zh, core), device_id_type=MESH)
            pl.when(zl != zt)(c.start)
    total = acc[0, 0, rem(3 * zl, NZL)]
    arrived("line", zrecv.at[pl.ds(1, NZL - 1)])
    for slot in range(1, NZL):
        total = total + decode(zrecv[slot])
    out[0, 0] = total

    for t in range(T):
        sent(t, gath[t].at[pl.ds(0, 7 * per)])
    sent(T, csend)
    for way in (0, 1):
        sent(T + 1 + way, ysend.at[way, pl.ds(2, 4 * NZL - 2)])
    sent(zs, zsend.at[pl.ds(1, NZL - 1)])
    assert len(names) <= NSEM


def on_device(activations, out_grad, tile_list, tile_count):
    tokens, feats = activations.shape
    n_mp = NX * 2
    ch = tokens // T
    tiles = pl.pallas_call(
        kernel,
        out_shape=jax.ShapeDtypeStruct((1, 1, BLK, BLK), jnp.float32),
        in_specs=[
            pl.BlockSpec(memory_space=pltpu.SMEM),
            pl.BlockSpec(memory_space=pl.ANY),
            pl.BlockSpec(memory_space=pl.ANY),
        ],
        out_specs=pl.BlockSpec(memory_space=pltpu.VMEM),
        scratch_shapes=[
            pltpu.VMEM((n_mp * feats // BLK, 2, BLK, ch // 2), jnp.bfloat16) for _ in range(T)
        ]
        + [
            pltpu.VMEM(activations.shape, jnp.bfloat16),
            pltpu.VMEM((out_grad.shape[1] // BLK, tokens, BLK), jnp.bfloat16),
            pltpu.VMEM((2, NY, NZL, BLK, BLK), jnp.float32),
            pltpu.VMEM((NY, NZL, CODE, BLK), jnp.int16),
            pltpu.VMEM((NY, NZL, CODE, BLK), jnp.int16),
            pltpu.VMEM((2, 4 * NZL, CODE, BLK), jnp.int16),
            pltpu.VMEM((2, 4, NZL, CODE, BLK), jnp.int16),
            pltpu.VMEM((NZL, CODE, BLK), jnp.int16),
            pltpu.VMEM((NZL, CODE, BLK), jnp.int16),
            pltpu.SemaphoreType.DMA((T + 1,)),
            pltpu.SemaphoreType.DMA((T + 4,)),
            pltpu.SemaphoreType.DMA((NSEM,)),
        ],
        compiler_params=pltpu.CompilerParams(
            collective_id=0, has_side_effects=True, vmem_limit_bytes=62 * 1024 * 1024
        ),
    )(jnp.swapaxes(tile_list, 1, 2), activations, out_grad)
    return jnp.where(lax.axis_index("dp") < tile_count[0], tiles, 0.0)


def solution(mesh):
    placed = (P("dp", "mp"), P("dp", "mp"), P("mp", None, None), P("mp"))
    return jax.shard_map(
        on_device, mesh=mesh, in_specs=placed, out_specs=P("mp", "dp", None, None), check_vma=False
    )
```

```python
import jax
import jax.numpy as jnp
from jax import lax
from jax.experimental import pallas as pl
from jax.experimental.pallas import tpu as pltpu
from jax.sharding import PartitionSpec as P

MESH = pl.DeviceIdType.MESH
BLK = 128
NX, NY, NZL = 4, 8, 4
T = 4
NSEM = 66


RANGE = 32000.0
CODE = BLK + 16


def encode(v):
    rows = v.reshape(BLK // 16, 16, BLK)
    peak = jnp.max(jnp.abs(rows), axis=0)
    e = jnp.ceil(jnp.log2(jnp.maximum(peak, 1e-30)))
    q = jnp.round(rows * (RANGE * jnp.exp2(-e))[None])
    return jnp.concatenate([q.reshape(BLK, BLK), e], axis=0).astype(jnp.int32).astype(jnp.int16)


def decode(code):
    v = code.astype(jnp.int32).astype(jnp.float32)
    scale = jnp.exp2(v[BLK:]) * (1.0 / RANGE)
    return (v[:BLK].reshape(BLK // 16, 16, BLK) * scale[None]).reshape(BLK, BLK)


def rem(a, b):
    return lax.rem(a, jnp.int32(b))


def div(a, b):
    return lax.div(a, jnp.int32(b))


def kernel(tl, act, grad, out, *scratch):
    gath = scratch[:T]
    araw, gbuf, acc, csend, crecv, ysend, yrecv, zsend, zrecv, lsem, ssem, rsem = scratch[T:]
    tokens, feats = act.shape
    ch = tokens // T
    hf = ch // 2
    cols = grad.shape[1] // BLK
    per = feats // BLK

    dp, mp = lax.axis_index("dp"), lax.axis_index("mp")
    core, y, zl = rem(dp, 2), rem(div(dp, 2), NY), div(dp, 2 * NY)
    x, zh = div(mp, 2), rem(mp, 2)

    def dev(x_, y_, zl_, zh_, core_):
        return ((zl_ * NY + y_) * 2 + core_, x_ * 2 + zh_)

    xr, xl = rem(x + 1, NX), rem(x + NX - 1, NX)
    right, left = dev(xr, y, zl, zh, core), dev(xl, y, zl, zh, core)
    across = dev(x, y, zl, 1 - zh, core)
    twin = dev(x, y, zl, zh, 1 - core)
    up, down = dev(x, rem(y + 1, NY), zl, zh, core), dev(x, rem(y + NY - 1, NY), zl, zh, core)

    barrier = pltpu.get_barrier_semaphore()
    peers = [across, right, left, twin, up, down]
    peers += [dev(x, y, rem(zl + d, NZL), zh, core) for d in range(1, NZL)]
    for p in peers:
        pl.semaphore_signal(barrier, inc=1, device_id=p, device_id_type=MESH)

    loc = []
    for t in range(T):
        c = pltpu.make_async_copy(act.at[pl.ds(t * ch, ch)], araw.at[pl.ds(t * ch, ch)], lsem.at[t])
        c.start()
        loc.append(c)
    for q in range(cols):
        pltpu.make_async_copy(grad.at[:, pl.ds(q * BLK, BLK)], gbuf.at[q], lsem.at[T]).start()

    def turn(t):
        loc[t].wait()
        for h in (0, 1):
            for b in range(per):
                part = araw[t * ch + h * hf : t * ch + (h + 1) * hf, b * BLK : (b + 1) * BLK]
                gath[t][mp * per + b, h] = part.T

    turn(0)
    pl.semaphore_wait(barrier, len(peers))

    names = {}

    def send(group, name, src, dst, to):
        i = names.setdefault(name, len(names))
        pltpu.make_async_remote_copy(
            src_ref=src, dst_ref=dst, send_sem=ssem.at[group], recv_sem=rsem.at[i],
            device_id=to, device_id_type=MESH).start()

    def arrived(name, dst):
        i = names.setdefault(name, len(names))
        pltpu.make_async_remote_copy(
            src_ref=dst, dst_ref=dst, send_sem=ssem.at[0], recv_sem=rsem.at[i],
            device_id=twin, device_id_type=MESH).wait_recv()

    def sent(group, ref):
        pltpu.make_async_remote_copy(
            src_ref=ref, dst_ref=ref, send_sem=ssem.at[group], recv_sem=rsem.at[0],
            device_id=twin, device_id_type=MESH).wait_send()

    mix = T - 1

    def whole(t, m):
        return gath[t].at[pl.ds(m * per, per)]

    def part(side, t, d, m):
        if side == "par" and t == mix:
            return gath[t].at[pl.ds(m * per + d * (per // 2), per // 2), 0]
        return gath[t].at[pl.ds(m * per, per), d]

    def spread(side, t, m):
        for h in (0, 1):
            for d, to in ((0, right), (1, left)):
                g = h if d == 0 else 1 - h
                name = (side, t, d) if h == 0 else (side, t)
                send(t, name, part(side, t, g, m), part(side, t, g, m), to)

    def pass_on(side, t):
        z = zh if side == "own" else 1 - zh
        for d, m, to in ((0, xl * 2 + z, right), (1, xr * 2 + z, left)):
            arrived((side, t, d), part(side, t, d, m))
            send(t, (side, t), part(side, t, d, m), part(side, t, d, m), to)

    def rest(side, t):
        n = per if side == "par" and t == mix else 2 * per
        arrived((side, t), gath[t].at[pl.ds(0, n)])

    def cross(t):
        m = x * 2 + 1 - zh
        arrived(("z", t), whole(t, m))
        spread("par", t, m)

    def group(t, cr, dy):
        for zp in range(NZL):
            zt = (3 * zp) % NZL
            k = (zt * NY + rem(y + dy, NY)) * 2 + rem(core + cr, 2)
            a = gath[t][tl[0, 0, k]]
            g = gbuf[rem(tl[0, 1, k], cols), pl.ds(t * ch, ch)]
            p = jnp.dot(jnp.concatenate([a[0], a[1]], axis=1), g, preferred_element_type=jnp.float32)
            acc[cr, dy, zp] = p if t == 0 else acc[cr, dy, zp] + p

    def multiply(t):
        @pl.loop(0, NY)
        def _(dy):
            group(t, 0, dy)
            group(t, 1, dy)

    def cross_own(t):
        send(t, ("z", t), whole(t, mp), whole(t, mp), across)

    cross_own(0)
    spread("own", 0, mp)
    for t in range(1, T):
        turn(t)
        spread("own", t, mp)
    pass_on("own", 0)
    cross_own(1)
    pass_on("own", 1)
    pass_on("own", 2)
    cross_own(2)
    pass_on("own", 3)
    cross_own(3)
    pltpu.make_async_copy(gbuf, gbuf, lsem.at[T]).wait()
    cross(0)
    cross(1)
    rest("own", mix)
    for x_ in (xl, xr, rem(x + 2, NX)):
        half = gath[mix].at[pl.ds((x_ * 2 + zh) * per, per), 1]
        send(mix, "late", half, half, across)
    pass_on("par", 0)
    cross(2)
    pass_on("par", 1)
    rest("own", 0)
    rest("par", 0)
    multiply(0)
    pass_on("par", 2)
    cross(3)
    rest("own", 1)
    rest("par", 1)
    multiply(1)
    pass_on("par", 3)
    rest("own", 2)
    rest("par", 2)
    multiply(2)
    rest("par", 3)
    arrived("late", gath[mix].at[pl.ds(0, 3 * per // 2)])

    def give(dy):
        group(T - 1, 1, dy)
        for zp in range(NZL):
            csend[dy, zp] = encode(acc[1, dy, zp])
        send(T, ("core", dy), csend.at[dy], crecv.at[dy], twin)

    def keep(dy):
        group(T - 1, 0, dy)

    def last(dy):
        give(dy)
        keep(dy)

    def ready(dy):
        arrived(("core", dy), crecv.at[dy])
        for zp in range(NZL):
            acc[0, dy, zp] = acc[0, dy, zp] + decode(crecv[dy, zp])

    def step(way, dist, zp):
        dy = dist if way == 0 else (NY - dist) % NY
        long = (zp >= 2) == (way == 0)
        v = acc[0, dy, zp]
        if dist < (4 if long else 3):
            arrived(("y", way, dist, zp), yrecv.at[way, dist, zp])
            v = v + decode(yrecv[way, dist, zp])
        ysend[way, (4 - dist) * NZL + (zp + 2 * (1 - way)) % NZL] = encode(v)
        send(
            T + 1 + way, ("y", way, dist - 1, zp),
            ysend.at[way, (4 - dist) * NZL + (zp + 2 * (1 - way)) % NZL],
            yrecv.at[way, dist - 1, zp], (up, down)[way])

    def steps(dist, part):
        for i in (0, 1):
            for way in (0, 1):
                step(way, dist, 2 * (part if way == 0 else 1 - part) + i)

    give(4)
    give(3)
    keep(4)
    give(5)
    keep(3)
    ready(4)
    steps(4, 1)
    keep(5)
    ready(3)
    ready(5)
    steps(3, 0)
    last(2)
    last(6)
    steps(3, 1)
    ready(2)
    ready(6)
    steps(2, 0)
    last(1)
    last(7)
    steps(2, 1)
    ready(1)
    ready(7)
    steps(1, 0)
    last(0)
    steps(1, 1)
    ready(0)

    zs = T + 3
    for part in (0, 1):
        for zp in (2 * part, 2 * part + 1):
            v = acc[0, 0, zp]
            for way in (0, 1):
                arrived(("y", way, 0, zp), yrecv.at[way, 0, zp])
                v = v + decode(yrecv[way, 0, zp])
            acc[0, 0, zp] = v
            zt = (3 * zp) % NZL
            slot = rem(zl - zt + NZL, NZL)
            zsend[zp] = encode(v)
            i = names.setdefault("line", len(names))
            c = pltpu.make_async_remote_copy(
                src_ref=zsend.at[zp], dst_ref=zrecv.at[slot], send_sem=ssem.at[zs],
                recv_sem=rsem.at[i], device_id=dev(x, y, zt, zh, core), device_id_type=MESH)
            pl.when(zl != zt)(c.start)
    total = acc[0, 0, rem(3 * zl, NZL)]
    arrived("line", zrecv.at[pl.ds(1, NZL - 1)])
    for slot in range(1, NZL):
        total = total + decode(zrecv[slot])
    out[0, 0] = total

    for t in range(T):
        sent(t, gath[t].at[pl.ds(0, 7 * per)])
    sent(T, csend)
    for way in (0, 1):
        sent(T + 1 + way, ysend.at[way, pl.ds(2, 4 * NZL - 2)])
    sent(zs, zsend.at[pl.ds(1, NZL - 1)])
    assert len(names) <= NSEM


def on_device(activations, out_grad, tile_list, tile_count):
    tokens, feats = activations.shape
    n_mp = NX * 2
    ch = tokens // T
    tiles = pl.pallas_call(
        kernel,
        out_shape=jax.ShapeDtypeStruct((1, 1, BLK, BLK), jnp.float32),
        in_specs=[
            pl.BlockSpec(memory_space=pltpu.SMEM),
            pl.BlockSpec(memory_space=pl.ANY),
            pl.BlockSpec(memory_space=pl.ANY),
        ],
        out_specs=pl.BlockSpec(memory_space=pltpu.VMEM),
        scratch_shapes=[
            pltpu.VMEM((n_mp * feats // BLK, 2, BLK, ch // 2), jnp.bfloat16) for _ in range(T)
        ]
        + [
            pltpu.VMEM(activations.shape, jnp.bfloat16),
            pltpu.VMEM((out_grad.shape[1] // BLK, tokens, BLK), jnp.bfloat16),
            pltpu.VMEM((2, NY, NZL, BLK, BLK), jnp.float32),
            pltpu.VMEM((NY, NZL, CODE, BLK), jnp.int16),
            pltpu.VMEM((NY, NZL, CODE, BLK), jnp.int16),
            pltpu.VMEM((2, 4 * NZL, CODE, BLK), jnp.int16),
            pltpu.VMEM((2, 4, NZL, CODE, BLK), jnp.int16),
            pltpu.VMEM((NZL, CODE, BLK), jnp.int16),
            pltpu.VMEM((NZL, CODE, BLK), jnp.int16),
            pltpu.SemaphoreType.DMA((T + 1,)),
            pltpu.SemaphoreType.DMA((T + 4,)),
            pltpu.SemaphoreType.DMA((NSEM,)),
        ],
        compiler_params=pltpu.CompilerParams(
            collective_id=0, has_side_effects=True, vmem_limit_bytes=62 * 1024 * 1024
        ),
    )(jnp.swapaxes(tile_list, 1, 2), activations, out_grad)
    return jnp.where(lax.axis_index("dp") < tile_count[0], tiles, 0.0)


def solution(mesh):
    placed = (P("dp", "mp"), P("dp", "mp"), P("mp", None, None), P("mp"))
    return jax.shard_map(
        on_device, mesh=mesh, in_specs=placed, out_specs=P("mp", "dp", None, None), check_vma=False
    )
```

```python
import jax
import jax.numpy as jnp
from jax import lax
from jax.experimental import pallas as pl
from jax.experimental.pallas import tpu as pltpu
from jax.sharding import PartitionSpec as P

MESH = pl.DeviceIdType.MESH
BLK = 128
NX, NY, NZL = 4, 8, 4
T = 4
NSEM = 81


RANGE = 32000.0
CODE = BLK + 16


def encode(v):
    rows = v.reshape(BLK // 16, 16, BLK)
    peak = jnp.max(jnp.abs(rows), axis=0)
    e = jnp.ceil(jnp.log2(jnp.maximum(peak, 1e-30)))
    q = jnp.round(rows * (RANGE * jnp.exp2(-e))[None])
    return jnp.concatenate([q.reshape(BLK, BLK), e], axis=0).astype(jnp.int32).astype(jnp.int16)


def decode(code):
    v = code.astype(jnp.int32).astype(jnp.float32)
    scale = jnp.exp2(v[BLK:]) * (1.0 / RANGE)
    return (v[:BLK].reshape(BLK // 16, 16, BLK) * scale[None]).reshape(BLK, BLK)


def rem(a, b):
    return lax.rem(a, jnp.int32(b))


def div(a, b):
    return lax.div(a, jnp.int32(b))


def kernel(tl, act, grad, out, *scratch):
    gath = scratch[:T]
    araw, gbuf, acc, csend, crecv, ysend, yrecv, zsend, zrecv, relay, late, lsem, ssem, rsem = scratch[T:]
    tokens, feats = act.shape
    ch = tokens // T
    hf = ch // 2
    cols = grad.shape[1] // BLK
    per = feats // BLK

    dp, mp = lax.axis_index("dp"), lax.axis_index("mp")
    core, y, zl = rem(dp, 2), rem(div(dp, 2), NY), div(dp, 2 * NY)
    x, zh = div(mp, 2), rem(mp, 2)

    def dev(x_, y_, zl_, zh_, core_):
        return ((zl_ * NY + y_) * 2 + core_, x_ * 2 + zh_)

    xr, xl = rem(x + 1, NX), rem(x + NX - 1, NX)
    right, left = dev(xr, y, zl, zh, core), dev(xl, y, zl, zh, core)
    zz = zh * NZL + zl

    def on_ring(q):
        q = rem(q + 2 * NZL, 2 * NZL)
        return dev(x, y, rem(q, NZL), div(q, NZL), core)

    ahead, behind = on_ring(zz + 1), on_ring(zz - 1)
    twin = dev(x, y, zl, zh, 1 - core)
    up, down = dev(x, rem(y + 1, NY), zl, zh, core), dev(x, rem(y + NY - 1, NY), zl, zh, core)

    barrier = pltpu.get_barrier_semaphore()
    peers = [ahead, behind, right, left, twin, up, down]
    peers += [dev(x, y, rem(zl + d, NZL), zh, core) for d in range(1, NZL)]
    for p in peers:
        pl.semaphore_signal(barrier, inc=1, device_id=p, device_id_type=MESH)

    loc = []
    for t in range(T):
        c = pltpu.make_async_copy(act.at[pl.ds(t * ch, ch)], araw.at[pl.ds(t * ch, ch)], lsem.at[t])
        c.start()
        loc.append(c)
    for q in range(cols):
        pltpu.make_async_copy(grad.at[:, pl.ds(q * BLK, BLK)], gbuf.at[q], lsem.at[T]).start()

    def turn(t):
        loc[t].wait()
        for h in (0, 1):
            for b in range(per):
                part = araw[t * ch + h * hf : t * ch + (h + 1) * hf, b * BLK : (b + 1) * BLK]
                gath[t][mp * per + b, h] = part.T

    turn(0)
    pl.semaphore_wait(barrier, len(peers))

    names = {}

    def send(group, name, src, dst, to):
        i = names.setdefault(name, len(names))
        pltpu.make_async_remote_copy(
            src_ref=src, dst_ref=dst, send_sem=ssem.at[group], recv_sem=rsem.at[i],
            device_id=to, device_id_type=MESH).start()

    def arrived(name, dst):
        i = names.setdefault(name, len(names))
        pltpu.make_async_remote_copy(
            src_ref=dst, dst_ref=dst, send_sem=ssem.at[0], recv_sem=rsem.at[i],
            device_id=twin, device_id_type=MESH).wait_recv()

    def sent(group, ref):
        pltpu.make_async_remote_copy(
            src_ref=ref, dst_ref=ref, send_sem=ssem.at[group], recv_sem=rsem.at[0],
            device_id=twin, device_id_type=MESH).wait_send()

    mix = T - 1

    def part(side, t, d, m):
        if side == "par" and t == mix:
            return gath[t].at[pl.ds(m * per + d * (per // 2), per // 2), 0]
        return gath[t].at[pl.ds(m * per, per), d]

    def spread(side, t, m):
        for h in (0, 1):
            for d, to in ((0, right), (1, left)):
                g = h if d == 0 else 1 - h
                name = (side, t, d) if h == 0 else (side, t)
                send(t, name, part(side, t, g, m), part(side, t, g, m), to)

    def pass_on(side, t):
        z = zh if side == "own" else 1 - zh
        for d, m, to in ((0, xl * 2 + z, right), (1, xr * 2 + z, left)):
            arrived((side, t, d), part(side, t, d, m))
            send(t, (side, t), part(side, t, d, m), part(side, t, d, m), to)

    def rest(side, t):
        n = per if side == "par" and t == mix else 2 * per
        arrived((side, t), gath[t].at[pl.ds(0, n)])

    def any_rows(n):
        return gath[0].at[pl.ds(0, n)]

    def final(way):
        return 1 - div(rem(zz + (1, 2 * NZL - 1)[way], 2 * NZL), NZL)

    def hop(t, s):
        if s > 1:
            arrived(("z", t, s - 1), any_rows(per))
        for way, to in ((0, ahead), (1, behind)):
            src = gath[t].at[pl.ds(mp * per, per), way] if s == 1 else relay.at[way, t, s - 2]
            dst = relay.at[way, t, s - 1] if s < 4 else gath[t].at[pl.ds((x * 2 + final(way)) * per, per), way]
            send(t if s == 1 else T + 4, ("z", t, s), src, dst, to)

    def late_hop(s):
        two = per // 2
        if s > 1:
            arrived(("late", s - 1), any_rows(3 * two))
        for way, to in ((0, ahead), (1, behind)):
            if s in (2, 3):
                send(T + 5, ("late", s), late.at[way, s - 2], late.at[way, s - 1], to)
                continue
            for j, x_ in enumerate((xl, xr, rem(x + 2, NX))):
                slot = pl.ds(j * two, two)
                if s == 1:
                    src = gath[mix].at[pl.ds((x_ * 2 + zh) * per + way * two, two), 1]
                    dst = late.at[way, 0, slot]
                else:
                    src = late.at[way, 2, slot]
                    dst = gath[mix].at[pl.ds((x_ * 2 + final(way)) * per + way * two, two), 1]
                send(T + 5, ("late", s), src, dst, to)

    def cross(t):
        arrived(("z", t, 4), any_rows(per))
        spread("par", t, x * 2 + 1 - zh)

    def group(t, cr, dy):
        for zp in range(NZL):
            zt = (3 * zp) % NZL
            k = (zt * NY + rem(y + dy, NY)) * 2 + rem(core + cr, 2)
            a = gath[t][tl[0, 0, k]]
            g = gbuf[rem(tl[0, 1, k], cols), pl.ds(t * ch, ch)]
            p = jnp.dot(jnp.concatenate([a[0], a[1]], axis=1), g, preferred_element_type=jnp.float32)
            acc[cr, dy, zp] = p if t == 0 else acc[cr, dy, zp] + p

    def multiply(t):
        @pl.loop(0, NY)
        def _(dy):
            group(t, 0, dy)
            group(t, 1, dy)

    hop(0, 1)
    spread("own", 0, mp)
    turn(1)
    hop(1, 1)
    spread("own", 1, mp)
    for t in range(2, T):
        turn(t)
        spread("own", t, mp)
    hop(0, 2)
    pass_on("own", 0)
    hop(1, 2)
    hop(0, 3)
    pass_on("own", 1)
    hop(1, 3)
    hop(0, 4)
    pass_on("own", 2)
    hop(1, 4)
    hop(2, 1)
    hop(3, 1)
    pass_on("own", 3)
    pltpu.make_async_copy(gbuf, gbuf, lsem.at[T]).wait()
    cross(0)
    cross(1)
    hop(2, 2)
    hop(3, 2)
    hop(2, 3)
    rest("own", mix)
    late_hop(1)
    hop(3, 3)
    pass_on("par", 0)
    hop(2, 4)
    hop(3, 4)
    late_hop(2)
    cross(2)
    pass_on("par", 1)
    late_hop(3)
    rest("own", 0)
    rest("par", 0)
    multiply(0)
    pass_on("par", 2)
    cross(3)
    late_hop(4)
    rest("own", 1)
    rest("par", 1)
    multiply(1)
    pass_on("par", 3)
    rest("own", 2)
    rest("par", 2)
    multiply(2)
    rest("par", 3)
    arrived(("late", 4), any_rows(3 * per // 2))

    def give(dy):
        group(T - 1, 1, dy)
        for zp in range(NZL):
            csend[dy, zp] = encode(acc[1, dy, zp])
        send(T, ("core", dy), csend.at[dy], crecv.at[dy], twin)

    def keep(dy):
        group(T - 1, 0, dy)

    def last(dy):
        give(dy)
        keep(dy)

    def ready(dy):
        arrived(("core", dy), crecv.at[dy])
        for zp in range(NZL):
            acc[0, dy, zp] = acc[0, dy, zp] + decode(crecv[dy, zp])

    def step(way, dist, zp):
        dy = dist if way == 0 else (NY - dist) % NY
        long = (zp >= 2) == (way == 0)
        v = acc[0, dy, zp]
        if dist < (4 if long else 3):
            arrived(("y", way, dist, zp), yrecv.at[way, dist, zp])
            v = v + decode(yrecv[way, dist, zp])
        ysend[way, (4 - dist) * NZL + (zp + 2 * (1 - way)) % NZL] = encode(v)
        send(
            T + 1 + way, ("y", way, dist - 1, zp),
            ysend.at[way, (4 - dist) * NZL + (zp + 2 * (1 - way)) % NZL],
            yrecv.at[way, dist - 1, zp], (up, down)[way])

    def steps(dist, part):
        for i in (0, 1):
            for way in (0, 1):
                step(way, dist, 2 * (part if way == 0 else 1 - part) + i)

    give(4)
    give(3)
    keep(4)
    give(5)
    keep(3)
    ready(4)
    steps(4, 1)
    keep(5)
    ready(3)
    ready(5)
    steps(3, 0)
    last(2)
    last(6)
    steps(3, 1)
    ready(2)
    ready(6)
    steps(2, 0)
    last(1)
    last(7)
    steps(2, 1)
    ready(1)
    ready(7)
    steps(1, 0)
    last(0)
    steps(1, 1)
    ready(0)

    zs = T + 3
    for part in (0, 1):
        for zp in (2 * part, 2 * part + 1):
            v = acc[0, 0, zp]
            for way in (0, 1):
                arrived(("y", way, 0, zp), yrecv.at[way, 0, zp])
                v = v + decode(yrecv[way, 0, zp])
            acc[0, 0, zp] = v
            zt = (3 * zp) % NZL
            slot = rem(zl - zt + NZL, NZL)
            zsend[zp] = encode(v)
            i = names.setdefault("line", len(names))
            c = pltpu.make_async_remote_copy(
                src_ref=zsend.at[zp], dst_ref=zrecv.at[slot], send_sem=ssem.at[zs],
                recv_sem=rsem.at[i], device_id=dev(x, y, zt, zh, core), device_id_type=MESH)
            pl.when(zl != zt)(c.start)
    total = acc[0, 0, rem(3 * zl, NZL)]
    arrived("line", zrecv.at[pl.ds(1, NZL - 1)])
    for slot in range(1, NZL):
        total = total + decode(zrecv[slot])
    out[0, 0] = total

    for t in range(T):
        sent(t, gath[t].at[pl.ds(0, (11 * per) // 2 if t == mix else 7 * per)])
    sent(T + 4, relay)
    sent(T + 5, any_rows(6 * per))
    sent(T, csend)
    for way in (0, 1):
        sent(T + 1 + way, ysend.at[way, pl.ds(2, 4 * NZL - 2)])
    sent(zs, zsend.at[pl.ds(1, NZL - 1)])
    assert len(names) <= NSEM


def on_device(activations, out_grad, tile_list, tile_count):
    tokens, feats = activations.shape
    n_mp = NX * 2
    ch = tokens // T
    tiles = pl.pallas_call(
        kernel,
        out_shape=jax.ShapeDtypeStruct((1, 1, BLK, BLK), jnp.float32),
        in_specs=[
            pl.BlockSpec(memory_space=pltpu.SMEM),
            pl.BlockSpec(memory_space=pl.ANY),
            pl.BlockSpec(memory_space=pl.ANY),
        ],
        out_specs=pl.BlockSpec(memory_space=pltpu.VMEM),
        scratch_shapes=[
            pltpu.VMEM((n_mp * feats // BLK, 2, BLK, ch // 2), jnp.bfloat16) for _ in range(T)
        ]
        + [
            pltpu.VMEM(activations.shape, jnp.bfloat16),
            pltpu.VMEM((out_grad.shape[1] // BLK, tokens, BLK), jnp.bfloat16),
            pltpu.VMEM((2, NY, NZL, BLK, BLK), jnp.float32),
            pltpu.VMEM((NY, NZL, CODE, BLK), jnp.int16),
            pltpu.VMEM((NY, NZL, CODE, BLK), jnp.int16),
            pltpu.VMEM((2, 4 * NZL, CODE, BLK), jnp.int16),
            pltpu.VMEM((2, 4, NZL, CODE, BLK), jnp.int16),
            pltpu.VMEM((NZL, CODE, BLK), jnp.int16),
            pltpu.VMEM((NZL, CODE, BLK), jnp.int16),
            pltpu.VMEM((2, T, 3, feats // BLK, BLK, ch // 2), jnp.bfloat16),
            pltpu.VMEM((2, 3, 3 * feats // BLK // 2, BLK, ch // 2), jnp.bfloat16),
            pltpu.SemaphoreType.DMA((T + 1,)),
            pltpu.SemaphoreType.DMA((T + 6,)),
            pltpu.SemaphoreType.DMA((NSEM,)),
        ],
        compiler_params=pltpu.CompilerParams(
            collective_id=0, has_side_effects=True, vmem_limit_bytes=62 * 1024 * 1024
        ),
    )(jnp.swapaxes(tile_list, 1, 2), activations, out_grad)
    return jnp.where(lax.axis_index("dp") < tile_count[0], tiles, 0.0)


def solution(mesh):
    placed = (P("dp", "mp"), P("dp", "mp"), P("mp", None, None), P("mp"))
    return jax.shard_map(
        on_device, mesh=mesh, in_specs=placed, out_specs=P("mp", "dp", None, None), check_vma=False
    )
```

```python
import jax
import jax.numpy as jnp
from jax import lax
from jax.experimental import pallas as pl
from jax.experimental.pallas import tpu as pltpu
from jax.sharding import PartitionSpec as P

MESH = pl.DeviceIdType.MESH
BLK = 128
NX, NY, NZL = 4, 8, 4
T = 4
NSEM = 81


RANGE = 32000.0
CODE = BLK + 16


def encode(v):
    rows = v.reshape(BLK // 16, 16, BLK)
    peak = jnp.max(jnp.abs(rows), axis=0)
    e = jnp.ceil(jnp.log2(jnp.maximum(peak, 1e-30)))
    q = jnp.round(rows * (RANGE * jnp.exp2(-e))[None])
    return jnp.concatenate([q.reshape(BLK, BLK), e], axis=0).astype(jnp.int32).astype(jnp.int16)


def decode(code):
    v = code.astype(jnp.int32).astype(jnp.float32)
    scale = jnp.exp2(v[BLK:]) * (1.0 / RANGE)
    return (v[:BLK].reshape(BLK // 16, 16, BLK) * scale[None]).reshape(BLK, BLK)


def rem(a, b):
    return lax.rem(a, jnp.int32(b))


def div(a, b):
    return lax.div(a, jnp.int32(b))


def kernel(tiles, act, grad, out, *scratch):
    gath = scratch[:T]
    araw, gbuf, acc, csend, crecv, ysend, yrecv, zsend, zrecv, relay, late, tl, lsem, ssem, rsem = scratch[T:]
    tokens, feats = act.shape
    ch = tokens // T
    hf = ch // 2
    cols = grad.shape[1] // BLK
    per = feats // BLK

    dp, mp = lax.axis_index("dp"), lax.axis_index("mp")
    core, y, zl = rem(dp, 2), rem(div(dp, 2), NY), div(dp, 2 * NY)
    x, zh = div(mp, 2), rem(mp, 2)

    def dev(x_, y_, zl_, zh_, core_):
        return ((zl_ * NY + y_) * 2 + core_, x_ * 2 + zh_)

    xr, xl = rem(x + 1, NX), rem(x + NX - 1, NX)
    right, left = dev(xr, y, zl, zh, core), dev(xl, y, zl, zh, core)
    zz = zh * NZL + zl

    def on_ring(q):
        q = rem(q + 2 * NZL, 2 * NZL)
        return dev(x, y, rem(q, NZL), div(q, NZL), core)

    ahead, behind = on_ring(zz + 1), on_ring(zz - 1)
    twin = dev(x, y, zl, zh, 1 - core)
    up, down = dev(x, rem(y + 1, NY), zl, zh, core), dev(x, rem(y + NY - 1, NY), zl, zh, core)

    loc = []
    for t in range(T):
        c = pltpu.make_async_copy(act.at[pl.ds(t * ch, ch)], araw.at[pl.ds(t * ch, ch)], lsem.at[t])
        c.start()
        loc.append(c)
    loc_tl = pltpu.make_async_copy(tiles, tl, lsem.at[T + 1])
    loc_tl.start()
    for q in range(cols):
        pltpu.make_async_copy(grad.at[:, pl.ds(q * BLK, BLK)], gbuf.at[q], lsem.at[T]).start()

    barrier = pltpu.get_barrier_semaphore()
    peers = [ahead, behind, right, left, twin, up, down]
    peers += [dev(x, y, rem(zl + d, NZL), zh, core) for d in range(1, NZL)]
    for p in peers:
        pl.semaphore_signal(barrier, inc=1, device_id=p, device_id_type=MESH)

    def turn(t):
        loc[t].wait()
        for h in (0, 1):
            for b in range(per):
                part = araw[t * ch + h * hf : t * ch + (h + 1) * hf, b * BLK : (b + 1) * BLK]
                gath[t][mp * per + b, h] = part.T

    turn(0)
    pl.semaphore_wait(barrier, len(peers))

    names = {}

    def send(group, name, src, dst, to):
        i = names.setdefault(name, len(names))
        pltpu.make_async_remote_copy(
            src_ref=src, dst_ref=dst, send_sem=ssem.at[group], recv_sem=rsem.at[i],
            device_id=to, device_id_type=MESH).start()

    def arrived(name, dst):
        i = names.setdefault(name, len(names))
        pltpu.make_async_remote_copy(
            src_ref=dst, dst_ref=dst, send_sem=ssem.at[0], recv_sem=rsem.at[i],
            device_id=twin, device_id_type=MESH).wait_recv()

    def sent(group, ref):
        pltpu.make_async_remote_copy(
            src_ref=ref, dst_ref=ref, send_sem=ssem.at[group], recv_sem=rsem.at[0],
            device_id=twin, device_id_type=MESH).wait_send()

    mix = T - 1

    def part(side, t, d, m):
        if side == "par" and t == mix:
            return gath[t].at[pl.ds(m * per + d * (per // 2), per // 2), 0]
        return gath[t].at[pl.ds(m * per, per), d]

    def spread(side, t, m):
        for h in (0, 1):
            for d, to in ((0, right), (1, left)):
                g = h if d == 0 else 1 - h
                name = (side, t, d) if h == 0 else (side, t)
                send(t, name, part(side, t, g, m), part(side, t, g, m), to)

    def pass_on(side, t):
        z = zh if side == "own" else 1 - zh
        for d, m, to in ((0, xl * 2 + z, right), (1, xr * 2 + z, left)):
            arrived((side, t, d), part(side, t, d, m))
            send(t, (side, t), part(side, t, d, m), part(side, t, d, m), to)

    def rest(side, t):
        n = per if side == "par" and t == mix else 2 * per
        arrived((side, t), gath[t].at[pl.ds(0, n)])

    def any_rows(n):
        return gath[0].at[pl.ds(0, n)]

    def final(way):
        return 1 - div(rem(zz + (1, 2 * NZL - 1)[way], 2 * NZL), NZL)

    def hop(t, s):
        if s > 1:
            arrived(("z", t, s - 1), any_rows(per))
        for way, to in ((0, ahead), (1, behind)):
            src = gath[t].at[pl.ds(mp * per, per), way] if s == 1 else relay.at[way, t, s - 2]
            dst = relay.at[way, t, s - 1] if s < 4 else gath[t].at[pl.ds((x * 2 + final(way)) * per, per), way]
            send(t if s == 1 else T + 4, ("z", t, s), src, dst, to)

    def late_hop(s):
        two = per // 2
        if s > 1:
            arrived(("late", s - 1), any_rows(3 * two))
        for way, to in ((0, ahead), (1, behind)):
            if s in (2, 3):
                send(T + 5, ("late", s), late.at[way, s - 2], late.at[way, s - 1], to)
                continue
            for j, x_ in enumerate((xl, xr, rem(x + 2, NX))):
                slot = pl.ds(j * two, two)
                if s == 1:
                    src = gath[mix].at[pl.ds((x_ * 2 + zh) * per + way * two, two), 1]
                    dst = late.at[way, 0, slot]
                else:
                    src = late.at[way, 2, slot]
                    dst = gath[mix].at[pl.ds((x_ * 2 + final(way)) * per + way * two, two), 1]
                send(T + 5, ("late", s), src, dst, to)

    def cross(t):
        arrived(("z", t, 4), any_rows(per))
        spread("par", t, x * 2 + 1 - zh)

    def group(t, cr, dy):
        for zp in range(NZL):
            zt = (3 * zp) % NZL
            k = (zt * NY + rem(y + dy, NY)) * 2 + rem(core + cr, 2)
            a = gath[t][tl[0, 0, k]]
            g = gbuf[rem(tl[0, 1, k], cols), pl.ds(t * ch, ch)]
            p = jnp.dot(jnp.concatenate([a[0], a[1]], axis=1), g, preferred_element_type=jnp.float32)
            acc[cr, dy, zp] = p if t == 0 else acc[cr, dy, zp] + p

    def multiply(t):
        @pl.loop(0, NY)
        def _(dy):
            group(t, 0, dy)
            group(t, 1, dy)

    hop(0, 1)
    spread("own", 0, mp)
    turn(1)
    hop(1, 1)
    spread("own", 1, mp)
    for t in range(2, T):
        turn(t)
        spread("own", t, mp)
    hop(0, 2)
    pass_on("own", 0)
    hop(1, 2)
    hop(0, 3)
    pass_on("own", 1)
    hop(1, 3)
    hop(0, 4)
    pass_on("own", 2)
    hop(1, 4)
    hop(2, 1)
    hop(3, 1)
    pass_on("own", 3)
    pltpu.make_async_copy(gbuf, gbuf, lsem.at[T]).wait()
    loc_tl.wait()
    cross(0)
    cross(1)
    hop(2, 2)
    hop(3, 2)
    hop(2, 3)
    rest("own", mix)
    hop(3, 3)
    late_hop(1)
    pass_on("par", 0)
    hop(2, 4)
    hop(3, 4)
    late_hop(2)
    cross(2)
    pass_on("par", 1)
    late_hop(3)
    rest("own", 0)
    rest("par", 0)
    multiply(0)
    pass_on("par", 2)
    cross(3)
    late_hop(4)
    rest("own", 1)
    rest("par", 1)
    multiply(1)
    pass_on("par", 3)
    rest("own", 2)
    rest("par", 2)
    multiply(2)
    rest("par", 3)
    arrived(("late", 4), any_rows(3 * per // 2))

    def give(dy):
        group(T - 1, 1, dy)
        for zp in range(NZL):
            csend[dy, zp] = encode(acc[1, dy, zp])
        send(T, ("core", dy), csend.at[dy], crecv.at[dy], twin)

    def keep(dy):
        group(T - 1, 0, dy)

    def last(dy):
        give(dy)
        keep(dy)

    def ready(dy):
        arrived(("core", dy), crecv.at[dy])
        for zp in range(NZL):
            acc[0, dy, zp] = acc[0, dy, zp] + decode(crecv[dy, zp])

    def step(way, dist, zp):
        dy = dist if way == 0 else (NY - dist) % NY
        long = (zp >= 2) == (way == 0)
        v = acc[0, dy, zp]
        if dist < (4 if long else 3):
            arrived(("y", way, dist, zp), yrecv.at[way, dist, zp])
            v = v + decode(yrecv[way, dist, zp])
        ysend[way, (4 - dist) * NZL + (zp + 2 * (1 - way)) % NZL] = encode(v)
        send(
            T + 1 + way, ("y", way, dist - 1, zp),
            ysend.at[way, (4 - dist) * NZL + (zp + 2 * (1 - way)) % NZL],
            yrecv.at[way, dist - 1, zp], (up, down)[way])

    def steps(dist, part):
        for i in (0, 1):
            for way in (0, 1):
                step(way, dist, 2 * (part if way == 0 else 1 - part) + i)

    give(4)
    give(3)
    keep(4)
    give(5)
    keep(3)
    ready(4)
    steps(4, 1)
    keep(5)
    ready(3)
    ready(5)
    steps(3, 0)
    last(2)
    last(6)
    steps(3, 1)
    ready(2)
    ready(6)
    steps(2, 0)
    last(1)
    last(7)
    steps(2, 1)
    ready(1)
    ready(7)
    steps(1, 0)
    last(0)
    steps(1, 1)
    ready(0)

    zs = T + 3
    for part in (0, 1):
        for zp in (2 * part, 2 * part + 1):
            v = acc[0, 0, zp]
            for way in (0, 1):
                arrived(("y", way, 0, zp), yrecv.at[way, 0, zp])
                v = v + decode(yrecv[way, 0, zp])
            acc[0, 0, zp] = v
            zt = (3 * zp) % NZL
            slot = rem(zl - zt + NZL, NZL)
            zsend[zp] = encode(v)
            i = names.setdefault("line", len(names))
            c = pltpu.make_async_remote_copy(
                src_ref=zsend.at[zp], dst_ref=zrecv.at[slot], send_sem=ssem.at[zs],
                recv_sem=rsem.at[i], device_id=dev(x, y, zt, zh, core), device_id_type=MESH)
            pl.when(zl != zt)(c.start)
    total = acc[0, 0, rem(3 * zl, NZL)]
    arrived("line", zrecv.at[pl.ds(1, NZL - 1)])
    for slot in range(1, NZL):
        total = total + decode(zrecv[slot])
    out[0, 0] = total

    for t in range(T):
        sent(t, gath[t].at[pl.ds(0, (11 * per) // 2 if t == mix else 7 * per)])
    sent(T + 4, relay)
    sent(T + 5, any_rows(6 * per))
    sent(T, csend)
    for way in (0, 1):
        sent(T + 1 + way, ysend.at[way, pl.ds(2, 4 * NZL - 2)])
    sent(zs, zsend.at[pl.ds(1, NZL - 1)])
    assert len(names) <= NSEM


def on_device(activations, out_grad, tile_list, tile_count):
    tokens, feats = activations.shape
    n_mp = NX * 2
    ch = tokens // T
    n_slots = tile_list.shape[1]
    tiles = pl.pallas_call(
        kernel,
        out_shape=jax.ShapeDtypeStruct((1, 1, BLK, BLK), jnp.float32),
        in_specs=[
            pl.BlockSpec(memory_space=pl.ANY),
            pl.BlockSpec(memory_space=pl.ANY),
            pl.BlockSpec(memory_space=pl.ANY),
        ],
        out_specs=pl.BlockSpec(memory_space=pltpu.VMEM),
        scratch_shapes=[
            pltpu.VMEM((n_mp * feats // BLK, 2, BLK, ch // 2), jnp.bfloat16) for _ in range(T)
        ]
        + [
            pltpu.VMEM(activations.shape, jnp.bfloat16),
            pltpu.VMEM((out_grad.shape[1] // BLK, tokens, BLK), jnp.bfloat16),
            pltpu.VMEM((2, NY, NZL, BLK, BLK), jnp.float32),
            pltpu.VMEM((NY, NZL, CODE, BLK), jnp.int16),
            pltpu.VMEM((NY, NZL, CODE, BLK), jnp.int16),
            pltpu.VMEM((2, 4 * NZL, CODE, BLK), jnp.int16),
            pltpu.VMEM((2, 4, NZL, CODE, BLK), jnp.int16),
            pltpu.VMEM((NZL, CODE, BLK), jnp.int16),
            pltpu.VMEM((NZL, CODE, BLK), jnp.int16),
            pltpu.VMEM((2, T, 3, feats // BLK, BLK, ch // 2), jnp.bfloat16),
            pltpu.VMEM((2, 3, 3 * feats // BLK // 2, BLK, ch // 2), jnp.bfloat16),
            pltpu.SMEM((1, 2, n_slots), jnp.int32),
            pltpu.SemaphoreType.DMA((T + 2,)),
            pltpu.SemaphoreType.DMA((T + 6,)),
            pltpu.SemaphoreType.DMA((NSEM,)),
        ],
        compiler_params=pltpu.CompilerParams(
            collective_id=0, has_side_effects=True, vmem_limit_bytes=62 * 1024 * 1024
        ),
    )(jnp.swapaxes(tile_list, 1, 2), activations, out_grad)
    return jnp.where(lax.axis_index("dp") < tile_count[0], tiles, 0.0)


def solution(mesh):
    placed = (P("dp", "mp"), P("dp", "mp"), P("mp", None, None), P("mp"))
    return jax.shard_map(
        on_device, mesh=mesh, in_specs=placed, out_specs=P("mp", "dp", None, None), check_vma=False
    )
```

```python
import jax
import jax.numpy as jnp
from jax import lax
from jax.experimental import pallas as pl
from jax.experimental.pallas import tpu as pltpu
from jax.sharding import PartitionSpec as P

MESH = pl.DeviceIdType.MESH
BLK = 128
NX, NY, NZL = 4, 8, 4
T = 4
NSEM = 81


RANGE = 32000.0
CODE = BLK + 16


def encode(v):
    rows = v.reshape(BLK // 16, 16, BLK)
    peak = jnp.max(jnp.abs(rows), axis=0)
    e = jnp.ceil(jnp.log2(jnp.maximum(peak, 1e-30)))
    q = jnp.round(rows * (RANGE * jnp.exp2(-e))[None])
    return jnp.concatenate([q.reshape(BLK, BLK), e], axis=0).astype(jnp.int32).astype(jnp.int16)


def decode(code):
    v = code.astype(jnp.int32).astype(jnp.float32)
    scale = jnp.exp2(v[BLK:]) * (1.0 / RANGE)
    return (v[:BLK].reshape(BLK // 16, 16, BLK) * scale[None]).reshape(BLK, BLK)


def rem(a, b):
    return lax.rem(a, jnp.int32(b))


def div(a, b):
    return lax.div(a, jnp.int32(b))


def kernel(tiles, act, grad, out, *scratch):
    gath = scratch[:T]
    araw, gbuf, acc, csend, crecv, ysend, yrecv, zsend, zrecv, relay, late, tl, lsem, ssem, rsem = scratch[T:]
    tokens, feats = act.shape
    ch = tokens // T
    hf = ch // 2
    cols = grad.shape[1] // BLK
    per = feats // BLK

    dp, mp = lax.axis_index("dp"), lax.axis_index("mp")
    core, y, zl = rem(dp, 2), rem(div(dp, 2), NY), div(dp, 2 * NY)
    x, zh = div(mp, 2), rem(mp, 2)

    def dev(x_, y_, zl_, zh_, core_):
        return ((zl_ * NY + y_) * 2 + core_, x_ * 2 + zh_)

    xr, xl = rem(x + 1, NX), rem(x + NX - 1, NX)
    right, left = dev(xr, y, zl, zh, core), dev(xl, y, zl, zh, core)
    zz = zh * NZL + zl

    def on_ring(q):
        q = rem(q + 2 * NZL, 2 * NZL)
        return dev(x, y, rem(q, NZL), div(q, NZL), core)

    ahead, behind = on_ring(zz + 1), on_ring(zz - 1)
    twin = dev(x, y, zl, zh, 1 - core)
    up, down = dev(x, rem(y + 1, NY), zl, zh, core), dev(x, rem(y + NY - 1, NY), zl, zh, core)

    loc = []
    for t in range(T):
        c = pltpu.make_async_copy(act.at[pl.ds(t * ch, ch)], araw.at[pl.ds(t * ch, ch)], lsem.at[t])
        c.start()
        loc.append(c)
    loc_tl = pltpu.make_async_copy(tiles, tl, lsem.at[T + 1])
    loc_tl.start()
    for q in range(cols):
        pltpu.make_async_copy(grad.at[:, pl.ds(q * BLK, BLK)], gbuf.at[q], lsem.at[T]).start()

    barrier = pltpu.get_barrier_semaphore()
    peers = [ahead, behind, right, left, twin, up, down]
    peers += [dev(x, y, rem(zl + d, NZL), zh, core) for d in range(1, NZL)]
    for p in peers:
        pl.semaphore_signal(barrier, inc=1, device_id=p, device_id_type=MESH)

    def turn(t):
        loc[t].wait()
        for h in (0, 1):
            for b in range(per):
                part = araw[t * ch + h * hf : t * ch + (h + 1) * hf, b * BLK : (b + 1) * BLK]
                gath[t][mp * per + b, h] = part.T

    turn(0)
    pl.semaphore_wait(barrier, len(peers))

    names = {}

    def send(group, name, src, dst, to):
        i = names.setdefault(name, len(names))
        pltpu.make_async_remote_copy(
            src_ref=src, dst_ref=dst, send_sem=ssem.at[group], recv_sem=rsem.at[i],
            device_id=to, device_id_type=MESH).start()

    def arrived(name, dst):
        i = names.setdefault(name, len(names))
        pltpu.make_async_remote_copy(
            src_ref=dst, dst_ref=dst, send_sem=ssem.at[0], recv_sem=rsem.at[i],
            device_id=twin, device_id_type=MESH).wait_recv()

    def sent(group, ref):
        pltpu.make_async_remote_copy(
            src_ref=ref, dst_ref=ref, send_sem=ssem.at[group], recv_sem=rsem.at[0],
            device_id=twin, device_id_type=MESH).wait_send()

    mix = T - 1

    def part(side, t, d, m):
        if side == "par" and t == mix:
            return gath[t].at[pl.ds(m * per + d * (per // 2), per // 2), 0]
        return gath[t].at[pl.ds(m * per, per), d]

    def spread(side, t, m):
        for h in (0, 1):
            for d, to in ((0, right), (1, left)):
                g = h if d == 0 else 1 - h
                name = (side, t, d) if h == 0 else (side, t)
                send(t, name, part(side, t, g, m), part(side, t, g, m), to)

    def pass_on(side, t):
        z = zh if side == "own" else 1 - zh
        for d, m, to in ((0, xl * 2 + z, right), (1, xr * 2 + z, left)):
            arrived((side, t, d), part(side, t, d, m))
            send(t, (side, t), part(side, t, d, m), part(side, t, d, m), to)

    def rest(side, t):
        n = per if side == "par" and t == mix else 2 * per
        arrived((side, t), gath[t].at[pl.ds(0, n)])

    def any_rows(n):
        return gath[0].at[pl.ds(0, n)]

    def final(way):
        return 1 - div(rem(zz + (1, 2 * NZL - 1)[way], 2 * NZL), NZL)

    def hop(t, s):
        if s > 1:
            arrived(("z", t, s - 1), any_rows(per))
        for way, to in ((0, ahead), (1, behind)):
            src = gath[t].at[pl.ds(mp * per, per), way] if s == 1 else relay.at[way, t, s - 2]
            dst = relay.at[way, t, s - 1] if s < 4 else gath[t].at[pl.ds((x * 2 + final(way)) * per, per), way]
            send(t if s == 1 else T + 4, ("z", t, s), src, dst, to)

    def late_hop(s):
        two = per // 2
        if s > 1:
            arrived(("late", s - 1), any_rows(3 * two))
        for way, to in ((0, ahead), (1, behind)):
            if s in (2, 3):
                send(T + 5, ("late", s), late.at[way, s - 2], late.at[way, s - 1], to)
                continue
            for j, x_ in enumerate((xl, xr, rem(x + 2, NX))):
                slot = pl.ds(j * two, two)
                if s == 1:
                    src = gath[mix].at[pl.ds((x_ * 2 + zh) * per + way * two, two), 1]
                    dst = late.at[way, 0, slot]
                else:
                    src = late.at[way, 2, slot]
                    dst = gath[mix].at[pl.ds((x_ * 2 + final(way)) * per + way * two, two), 1]
                send(T + 5, ("late", s), src, dst, to)

    def cross(t):
        arrived(("z", t, 4), any_rows(per))
        spread("par", t, x * 2 + 1 - zh)

    def group(t, cr, dy):
        for zp in range(NZL):
            zt = (3 * zp) % NZL
            k = (zt * NY + rem(y + dy, NY)) * 2 + rem(core + cr, 2)
            a = gath[t][tl[0, 0, k]]
            g = gbuf[rem(tl[0, 1, k], cols), pl.ds(t * ch, ch)]
            p = jnp.dot(jnp.concatenate([a[0], a[1]], axis=1), g, preferred_element_type=jnp.float32)
            acc[cr, dy, zp] = p if t == 0 else acc[cr, dy, zp] + p

    def multiply(t):
        @pl.loop(0, NY)
        def _(dy):
            group(t, 0, dy)
            group(t, 1, dy)

    hop(0, 1)
    spread("own", 0, mp)
    turn(1)
    hop(1, 1)
    spread("own", 1, mp)
    for t in range(2, T):
        turn(t)
        spread("own", t, mp)
    hop(0, 2)
    pass_on("own", 0)
    hop(1, 2)
    hop(0, 3)
    pass_on("own", 1)
    hop(1, 3)
    hop(0, 4)
    pass_on("own", 2)
    hop(1, 4)
    hop(2, 1)
    hop(3, 1)
    pass_on("own", 3)
    pltpu.make_async_copy(gbuf, gbuf, lsem.at[T]).wait()
    loc_tl.wait()
    cross(0)
    cross(1)
    hop(2, 2)
    hop(3, 2)
    hop(2, 3)
    rest("own", mix)
    hop(3, 3)
    late_hop(1)
    pass_on("par", 0)
    hop(2, 4)
    hop(3, 4)
    late_hop(2)
    cross(2)
    pass_on("par", 1)
    cross(3)
    pass_on("par", 2)
    late_hop(3)
    rest("own", 0)
    rest("par", 0)
    multiply(0)
    pass_on("par", 3)
    late_hop(4)
    rest("own", 1)
    rest("par", 1)
    multiply(1)
    rest("own", 2)
    rest("par", 2)
    multiply(2)
    rest("par", 3)
    arrived(("late", 4), any_rows(3 * per // 2))

    def give(dy):
        group(T - 1, 1, dy)
        for zp in range(NZL):
            csend[dy, zp] = encode(acc[1, dy, zp])
        send(T, ("core", dy), csend.at[dy], crecv.at[dy], twin)

    def keep(dy):
        group(T - 1, 0, dy)

    def last(dy):
        give(dy)
        keep(dy)

    def ready(dy):
        arrived(("core", dy), crecv.at[dy])
        for zp in range(NZL):
            acc[0, dy, zp] = acc[0, dy, zp] + decode(crecv[dy, zp])

    def step(way, dist, zp):
        dy = dist if way == 0 else (NY - dist) % NY
        long = (zp >= 2) == (way == 0)
        v = acc[0, dy, zp]
        if dist < (4 if long else 3):
            arrived(("y", way, dist, zp), yrecv.at[way, dist, zp])
            v = v + decode(yrecv[way, dist, zp])
        ysend[way, (4 - dist) * NZL + (zp + 2 * (1 - way)) % NZL] = encode(v)
        send(
            T + 1 + way, ("y", way, dist - 1, zp),
            ysend.at[way, (4 - dist) * NZL + (zp + 2 * (1 - way)) % NZL],
            yrecv.at[way, dist - 1, zp], (up, down)[way])

    def steps(dist, part):
        for i in (0, 1):
            for way in (0, 1):
                step(way, dist, 2 * (part if way == 0 else 1 - part) + i)

    give(4)
    give(3)
    keep(4)
    give(5)
    ready(4)
    steps(4, 1)
    keep(3)
    keep(5)
    ready(3)
    ready(5)
    steps(3, 0)
    for dy in (2, 6, 1, 7, 0):
        last(dy)
    steps(3, 1)
    ready(2)
    ready(6)
    steps(2, 0)
    steps(2, 1)
    ready(1)
    ready(7)
    steps(1, 0)
    steps(1, 1)
    ready(0)

    zs = T + 3
    for part in (0, 1):
        for zp in (2 * part, 2 * part + 1):
            v = acc[0, 0, zp]
            for way in (0, 1):
                arrived(("y", way, 0, zp), yrecv.at[way, 0, zp])
                v = v + decode(yrecv[way, 0, zp])
            acc[0, 0, zp] = v
            zt = (3 * zp) % NZL
            slot = rem(zl - zt + NZL, NZL)
            zsend[zp] = encode(v)
            i = names.setdefault("line", len(names))
            c = pltpu.make_async_remote_copy(
                src_ref=zsend.at[zp], dst_ref=zrecv.at[slot], send_sem=ssem.at[zs],
                recv_sem=rsem.at[i], device_id=dev(x, y, zt, zh, core), device_id_type=MESH)
            pl.when(zl != zt)(c.start)
    total = acc[0, 0, rem(3 * zl, NZL)]
    arrived("line", zrecv.at[pl.ds(1, NZL - 1)])
    for slot in range(1, NZL):
        total = total + decode(zrecv[slot])
    out[0, 0] = total

    for t in range(T):
        sent(t, gath[t].at[pl.ds(0, (11 * per) // 2 if t == mix else 7 * per)])
    sent(T + 4, relay)
    sent(T + 5, any_rows(6 * per))
    sent(T, csend)
    for way in (0, 1):
        sent(T + 1 + way, ysend.at[way, pl.ds(2, 4 * NZL - 2)])
    sent(zs, zsend.at[pl.ds(1, NZL - 1)])
    assert len(names) <= NSEM


def on_device(activations, out_grad, tile_list, tile_count):
    tokens, feats = activations.shape
    n_mp = NX * 2
    ch = tokens // T
    n_slots = tile_list.shape[1]
    tiles = pl.pallas_call(
        kernel,
        out_shape=jax.ShapeDtypeStruct((1, 1, BLK, BLK), jnp.float32),
        in_specs=[
            pl.BlockSpec(memory_space=pl.ANY),
            pl.BlockSpec(memory_space=pl.ANY),
            pl.BlockSpec(memory_space=pl.ANY),
        ],
        out_specs=pl.BlockSpec(memory_space=pltpu.VMEM),
        scratch_shapes=[
            pltpu.VMEM((n_mp * feats // BLK, 2, BLK, ch // 2), jnp.bfloat16) for _ in range(T)
        ]
        + [
            pltpu.VMEM(activations.shape, jnp.bfloat16),
            pltpu.VMEM((out_grad.shape[1] // BLK, tokens, BLK), jnp.bfloat16),
            pltpu.VMEM((2, NY, NZL, BLK, BLK), jnp.float32),
            pltpu.VMEM((NY, NZL, CODE, BLK), jnp.int16),
            pltpu.VMEM((NY, NZL, CODE, BLK), jnp.int16),
            pltpu.VMEM((2, 4 * NZL, CODE, BLK), jnp.int16),
            pltpu.VMEM((2, 4, NZL, CODE, BLK), jnp.int16),
            pltpu.VMEM((NZL, CODE, BLK), jnp.int16),
            pltpu.VMEM((NZL, CODE, BLK), jnp.int16),
            pltpu.VMEM((2, T, 3, feats // BLK, BLK, ch // 2), jnp.bfloat16),
            pltpu.VMEM((2, 3, 3 * feats // BLK // 2, BLK, ch // 2), jnp.bfloat16),
            pltpu.SMEM((1, 2, n_slots), jnp.int32),
            pltpu.SemaphoreType.DMA((T + 2,)),
            pltpu.SemaphoreType.DMA((T + 6,)),
            pltpu.SemaphoreType.DMA((NSEM,)),
        ],
        compiler_params=pltpu.CompilerParams(
            collective_id=0, has_side_effects=True, vmem_limit_bytes=62 * 1024 * 1024
        ),
    )(jnp.swapaxes(tile_list, 1, 2), activations, out_grad)
    return jnp.where(lax.axis_index("dp") < tile_count[0], tiles, 0.0)


def solution(mesh):
    placed = (P("dp", "mp"), P("dp", "mp"), P("mp", None, None), P("mp"))
    return jax.shard_map(
        on_device, mesh=mesh, in_specs=placed, out_specs=P("mp", "dp", None, None), check_vma=False
    )
```

```python
import jax
import jax.numpy as jnp
from jax import lax
from jax.experimental import pallas as pl
from jax.experimental.pallas import tpu as pltpu
from jax.sharding import PartitionSpec as P

MESH = pl.DeviceIdType.MESH
BLK = 128
NX, NY, NZL = 4, 8, 4
T = 4
NSEM = 81


RANGE = 32000.0
CODE = BLK + 16


def encode(v):
    rows = v.reshape(BLK // 16, 16, BLK)
    peak = jnp.max(jnp.abs(rows), axis=0)
    e = jnp.ceil(jnp.log2(jnp.maximum(peak, 1e-30)))
    q = jnp.round(rows * (RANGE * jnp.exp2(-e))[None])
    return jnp.concatenate([q.reshape(BLK, BLK), e], axis=0).astype(jnp.int32).astype(jnp.int16)


def decode(code):
    v = code.astype(jnp.int32).astype(jnp.float32)
    scale = jnp.exp2(v[BLK:]) * (1.0 / RANGE)
    return (v[:BLK].reshape(BLK // 16, 16, BLK) * scale[None]).reshape(BLK, BLK)


def rem(a, b):
    return lax.rem(a, jnp.int32(b))


def div(a, b):
    return lax.div(a, jnp.int32(b))


def kernel(tiles, act, grad, out, *scratch):
    gath = scratch[:T]
    araw, gbuf, acc, csend, crecv, ysend, yrecv, zsend, zrecv, relay, late, tl, lsem, ssem, rsem = scratch[T:]
    tokens, feats = act.shape
    ch = tokens // T
    hf = ch // 2
    cols = grad.shape[1] // BLK
    per = feats // BLK

    dp, mp = lax.axis_index("dp"), lax.axis_index("mp")
    core, y, zl = rem(dp, 2), rem(div(dp, 2), NY), div(dp, 2 * NY)
    x, zh = div(mp, 2), rem(mp, 2)

    def dev(x_, y_, zl_, zh_, core_):
        return ((zl_ * NY + y_) * 2 + core_, x_ * 2 + zh_)

    xr, xl = rem(x + 1, NX), rem(x + NX - 1, NX)
    right, left = dev(xr, y, zl, zh, core), dev(xl, y, zl, zh, core)
    zz = zh * NZL + zl

    def on_ring(q):
        q = rem(q + 2 * NZL, 2 * NZL)
        return dev(x, y, rem(q, NZL), div(q, NZL), core)

    ahead, behind = on_ring(zz + 1), on_ring(zz - 1)
    twin = dev(x, y, zl, zh, 1 - core)
    up, down = dev(x, rem(y + 1, NY), zl, zh, core), dev(x, rem(y + NY - 1, NY), zl, zh, core)

    loc = []
    for t in range(T):
        c = pltpu.make_async_copy(act.at[pl.ds(t * ch, ch)], araw.at[pl.ds(t * ch, ch)], lsem.at[t])
        c.start()
        loc.append(c)
    loc_tl = pltpu.make_async_copy(tiles, tl, lsem.at[T + 1])
    loc_tl.start()
    for q in range(cols):
        pltpu.make_async_copy(grad.at[:, pl.ds(q * BLK, BLK)], gbuf.at[q], lsem.at[T]).start()

    barrier = pltpu.get_barrier_semaphore()
    peers = [ahead, behind, right, left, twin, up, down]
    peers += [dev(x, y, rem(zl + d, NZL), zh, core) for d in range(1, NZL)]
    for p in peers:
        pl.semaphore_signal(barrier, inc=1, device_id=p, device_id_type=MESH)

    def turn(t):
        loc[t].wait()
        for h in (0, 1):
            for b in range(per):
                part = araw[t * ch + h * hf : t * ch + (h + 1) * hf, b * BLK : (b + 1) * BLK]
                gath[t][mp * per + b, h] = part.T

    turn(0)
    pl.semaphore_wait(barrier, len(peers))

    names = {}

    def send(group, name, src, dst, to):
        i = names.setdefault(name, len(names))
        pltpu.make_async_remote_copy(
            src_ref=src, dst_ref=dst, send_sem=ssem.at[group], recv_sem=rsem.at[i],
            device_id=to, device_id_type=MESH).start()

    def arrived(name, dst):
        i = names.setdefault(name, len(names))
        pltpu.make_async_remote_copy(
            src_ref=dst, dst_ref=dst, send_sem=ssem.at[0], recv_sem=rsem.at[i],
            device_id=twin, device_id_type=MESH).wait_recv()

    def sent(group, ref):
        pltpu.make_async_remote_copy(
            src_ref=ref, dst_ref=ref, send_sem=ssem.at[group], recv_sem=rsem.at[0],
            device_id=twin, device_id_type=MESH).wait_send()

    mix = T - 1

    def part(side, t, d, m):
        if side == "par" and t == mix:
            return gath[t].at[pl.ds(m * per + d * (per // 2), per // 2), 0]
        return gath[t].at[pl.ds(m * per, per), d]

    def spread(side, t, m):
        for h in (0, 1):
            for d, to in ((0, right), (1, left)):
                g = h if d == 0 else 1 - h
                name = (side, t, d) if h == 0 else (side, t)
                send(t, name, part(side, t, g, m), part(side, t, g, m), to)

    def pass_on(side, t):
        z = zh if side == "own" else 1 - zh
        for d, m, to in ((0, xl * 2 + z, right), (1, xr * 2 + z, left)):
            arrived((side, t, d), part(side, t, d, m))
            send(t, (side, t), part(side, t, d, m), part(side, t, d, m), to)

    def rest(side, t):
        n = per if side == "par" and t == mix else 2 * per
        arrived((side, t), gath[t].at[pl.ds(0, n)])

    def any_rows(n):
        return gath[0].at[pl.ds(0, n)]

    def final(way):
        return 1 - div(rem(zz + (1, 2 * NZL - 1)[way], 2 * NZL), NZL)

    def hop(t, s):
        if s > 1:
            arrived(("z", t, s - 1), any_rows(per))
        for way, to in ((0, ahead), (1, behind)):
            src = gath[t].at[pl.ds(mp * per, per), way] if s == 1 else relay.at[way, t, s - 2]
            dst = relay.at[way, t, s - 1] if s < 4 else gath[t].at[pl.ds((x * 2 + final(way)) * per, per), way]
            send(t if s == 1 else T + 4, ("z", t, s), src, dst, to)

    def late_hop(s):
        two = per // 2
        if s > 1:
            arrived(("late", s - 1), any_rows(3 * two))
        for way, to in ((0, ahead), (1, behind)):
            if s in (2, 3):
                send(T + 5, ("late", s), late.at[way, s - 2], late.at[way, s - 1], to)
                continue
            for j, x_ in enumerate((xl, xr, rem(x + 2, NX))):
                slot = pl.ds(j * two, two)
                if s == 1:
                    src = gath[mix].at[pl.ds((x_ * 2 + zh) * per + way * two, two), 1]
                    dst = late.at[way, 0, slot]
                else:
                    src = late.at[way, 2, slot]
                    dst = gath[mix].at[pl.ds((x_ * 2 + final(way)) * per + way * two, two), 1]
                send(T + 5, ("late", s), src, dst, to)

    def cross(t):
        arrived(("z", t, 4), any_rows(per))
        spread("par", t, x * 2 + 1 - zh)

    def group(t, cr, dy):
        for zp in range(NZL):
            zt = (3 * zp) % NZL
            k = (zt * NY + rem(y + dy, NY)) * 2 + rem(core + cr, 2)
            a = gath[t][tl[0, 0, k]]
            g = gbuf[rem(tl[0, 1, k], cols), pl.ds(t * ch, ch)]
            p = jnp.dot(jnp.concatenate([a[0], a[1]], axis=1), g, preferred_element_type=jnp.float32)
            acc[cr, dy, zp] = p if t == 0 else acc[cr, dy, zp] + p

    def multiply(t):
        @pl.loop(0, NY)
        def _(dy):
            group(t, 0, dy)
            group(t, 1, dy)

    hop(0, 1)
    spread("own", 0, mp)
    turn(1)
    hop(1, 1)
    spread("own", 1, mp)
    for t in range(2, T):
        turn(t)
        spread("own", t, mp)
    hop(0, 2)
    pass_on("own", 0)
    hop(1, 2)
    hop(0, 3)
    pass_on("own", 1)
    hop(1, 3)
    hop(0, 4)
    pass_on("own", 2)
    hop(1, 4)
    hop(2, 1)
    hop(3, 1)
    pass_on("own", 3)
    pltpu.make_async_copy(gbuf, gbuf, lsem.at[T]).wait()
    loc_tl.wait()
    cross(0)
    cross(1)
    hop(2, 2)
    hop(3, 2)
    hop(2, 3)
    rest("own", mix)
    hop(3, 3)
    late_hop(1)
    pass_on("par", 0)
    hop(2, 4)
    hop(3, 4)
    late_hop(2)
    cross(2)
    pass_on("par", 1)
    cross(3)
    late_hop(3)
    pass_on("par", 2)
    rest("own", 0)
    rest("par", 0)
    multiply(0)
    rest("own", 1)
    rest("par", 1)
    multiply(1)
    pass_on("par", 3)
    late_hop(4)
    rest("own", 2)
    rest("par", 2)
    multiply(2)
    rest("par", 3)
    arrived(("late", 4), any_rows(3 * per // 2))

    def give(dy):
        group(T - 1, 1, dy)
        for zp in range(NZL):
            csend[dy, zp] = encode(acc[1, dy, zp])
        send(T, ("core", dy), csend.at[dy], crecv.at[dy], twin)

    def keep(dy):
        group(T - 1, 0, dy)

    def last(dy):
        give(dy)
        keep(dy)

    def ready(dy):
        arrived(("core", dy), crecv.at[dy])
        for zp in range(NZL):
            acc[0, dy, zp] = acc[0, dy, zp] + decode(crecv[dy, zp])

    def step(way, dist, zp):
        dy = dist if way == 0 else (NY - dist) % NY
        long = (zp >= 2) == (way == 0)
        v = acc[0, dy, zp]
        if dist < (4 if long else 3):
            arrived(("y", way, dist, zp), yrecv.at[way, dist, zp])
            v = v + decode(yrecv[way, dist, zp])
        ysend[way, (4 - dist) * NZL + (zp + 2 * (1 - way)) % NZL] = encode(v)
        send(
            T + 1 + way, ("y", way, dist - 1, zp),
            ysend.at[way, (4 - dist) * NZL + (zp + 2 * (1 - way)) % NZL],
            yrecv.at[way, dist - 1, zp], (up, down)[way])

    def steps(dist, part):
        for i in (0, 1):
            for way in (0, 1):
                step(way, dist, 2 * (part if way == 0 else 1 - part) + i)

    give(4)
    give(3)
    keep(4)
    give(5)
    ready(4)
    steps(4, 1)
    keep(3)
    keep(5)
    ready(3)
    ready(5)
    steps(3, 0)
    for dy in (2, 6, 1, 7, 0):
        last(dy)
    steps(3, 1)
    ready(2)
    ready(6)
    steps(2, 0)
    steps(2, 1)
    ready(1)
    ready(7)
    steps(1, 0)
    steps(1, 1)
    ready(0)

    zs = T + 3
    for part in (0, 1):
        for zp in (2 * part, 2 * part + 1):
            v = acc[0, 0, zp]
            for way in (0, 1):
                arrived(("y", way, 0, zp), yrecv.at[way, 0, zp])
                v = v + decode(yrecv[way, 0, zp])
            acc[0, 0, zp] = v
            zt = (3 * zp) % NZL
            slot = rem(zl - zt + NZL, NZL)
            zsend[zp] = encode(v)
            i = names.setdefault("line", len(names))
            c = pltpu.make_async_remote_copy(
                src_ref=zsend.at[zp], dst_ref=zrecv.at[slot], send_sem=ssem.at[zs],
                recv_sem=rsem.at[i], device_id=dev(x, y, zt, zh, core), device_id_type=MESH)
            pl.when(zl != zt)(c.start)
    total = acc[0, 0, rem(3 * zl, NZL)]
    arrived("line", zrecv.at[pl.ds(1, NZL - 1)])
    for slot in range(1, NZL):
        total = total + decode(zrecv[slot])
    out[0, 0] = total

    for t in range(T):
        sent(t, gath[t].at[pl.ds(0, (11 * per) // 2 if t == mix else 7 * per)])
    sent(T + 4, relay)
    sent(T + 5, any_rows(6 * per))
    sent(T, csend)
    for way in (0, 1):
        sent(T + 1 + way, ysend.at[way, pl.ds(2, 4 * NZL - 2)])
    sent(zs, zsend.at[pl.ds(1, NZL - 1)])
    assert len(names) <= NSEM


def on_device(activations, out_grad, tile_list, tile_count):
    tokens, feats = activations.shape
    n_mp = NX * 2
    ch = tokens // T
    n_slots = tile_list.shape[1]
    tiles = pl.pallas_call(
        kernel,
        out_shape=jax.ShapeDtypeStruct((1, 1, BLK, BLK), jnp.float32),
        in_specs=[
            pl.BlockSpec(memory_space=pl.ANY),
            pl.BlockSpec(memory_space=pl.ANY),
            pl.BlockSpec(memory_space=pl.ANY),
        ],
        out_specs=pl.BlockSpec(memory_space=pltpu.VMEM),
        scratch_shapes=[
            pltpu.VMEM((n_mp * feats // BLK, 2, BLK, ch // 2), jnp.bfloat16) for _ in range(T)
        ]
        + [
            pltpu.VMEM(activations.shape, jnp.bfloat16),
            pltpu.VMEM((out_grad.shape[1] // BLK, tokens, BLK), jnp.bfloat16),
            pltpu.VMEM((2, NY, NZL, BLK, BLK), jnp.float32),
            pltpu.VMEM((NY, NZL, CODE, BLK), jnp.int16),
            pltpu.VMEM((NY, NZL, CODE, BLK), jnp.int16),
            pltpu.VMEM((2, 4 * NZL, CODE, BLK), jnp.int16),
            pltpu.VMEM((2, 4, NZL, CODE, BLK), jnp.int16),
            pltpu.VMEM((NZL, CODE, BLK), jnp.int16),
            pltpu.VMEM((NZL, CODE, BLK), jnp.int16),
            pltpu.VMEM((2, T, 3, feats // BLK, BLK, ch // 2), jnp.bfloat16),
            pltpu.VMEM((2, 3, 3 * feats // BLK // 2, BLK, ch // 2), jnp.bfloat16),
            pltpu.SMEM((1, 2, n_slots), jnp.int32),
            pltpu.SemaphoreType.DMA((T + 2,)),
            pltpu.SemaphoreType.DMA((T + 6,)),
            pltpu.SemaphoreType.DMA((NSEM,)),
        ],
        compiler_params=pltpu.CompilerParams(
            collective_id=0, has_side_effects=True, vmem_limit_bytes=62 * 1024 * 1024
        ),
    )(jnp.swapaxes(tile_list, 1, 2), activations, out_grad)
    return jnp.where(lax.axis_index("dp") < tile_count[0], tiles, 0.0)


def solution(mesh):
    placed = (P("dp", "mp"), P("dp", "mp"), P("mp", None, None), P("mp"))
    return jax.shard_map(
        on_device, mesh=mesh, in_specs=placed, out_specs=P("mp", "dp", None, None), check_vma=False
    )
```
